256 devices in a mesh: ctx: 32 (over y, x, core), head: 8 (over z).
Axes of the slice: x: 4, y: 4, z: 8, core: 2. Of those that a mesh axis runs over, the one named last changes fastest.
Arguments:
- queries: float32 [16384, 8192], P('ctx', 'head'), as said below
- keys: float32 [16384, 8192], P('ctx', 'head')
- values: float32 [16384, 8192], P('ctx', 'head')
- head_gain: float32 [2, 64], P(None, 'head'), may hold values from 0.3 to 3
Outputs:
- mixed: float32 [16384, 8192], P('ctx', 'head')
The draws below stay inside these ranges and needn't reach their ends.
Inputs may be any that keep to these rules, and one draw needn't show every extreme that they name: queries, keys and values are finite real numbers.
All inputs are finite; a program needn't handle non-finite values.
Results may differ from the reference program's by a relative error of at most 0.0003.
Values sent between devices are 32-bit elements; how exact they have to be, the bound alone decides.
A program may use at most 64 MiB of HBM per device.

```python
import math
import jax
import jax.numpy as jnp
from jax import lax

HEADS = 64
HD = 128
WINDOW = 128
TOKENS = 16384


def paired_draw(key):
    columns = HEADS * HD
    query_part = jnp.clip(jax.random.normal(jax.random.fold_in(key, 101), (TOKENS, columns), jnp.float32), -6.0, 6.0)
    key_part = jnp.clip(jax.random.normal(jax.random.fold_in(key, 102), (TOKENS, columns), jnp.float32), -6.0, 6.0)
    return (query_part, key_part)


def draw_queries(key, part):
    return paired_draw(key)[0]


def draw_keys(key, part):
    return paired_draw(key)[1]


def draw_values(key, part):
    columns = HEADS * HD
    base_values = jnp.clip(jax.random.normal(jax.random.fold_in(key, 201), (TOKENS, columns), jnp.float32), -6.0, 6.0)
    return base_values


def shard_levels(rng, dims, shards, smallest, high):
    loudness = 1.0
    for position, parts in shards:
        draws = jax.random.uniform(jax.random.fold_in(jax.random.fold_in(rng, 6), position), (parts,), jnp.float32, smallest / len(shards), high / len(shards))
        loudness = loudness * jnp.repeat(jnp.exp(draws), dims[position] // parts).reshape((-1,) + (1,) * (len(dims) - 1 - position))
    return loudness


def setup_inputs(seed: int = 0) -> dict:
    key_of = jax.random.split(jax.random.key(seed), 5)
    return {
        "queries": draw_queries(jax.random.fold_in(key_of[4], 71), 0),
        "keys": draw_keys(jax.random.fold_in(key_of[4], 71), 0),
        "values": draw_values(jax.random.fold_in(key_of[4], 71), 0),
        "head_gain": jnp.clip(jnp.exp(math.log(3.0) - 2.3025851 * jax.random.uniform(key_of[3], (2, HEADS), jnp.float32) ** shard_levels(key_of[3], (2, HEADS), ((1, 8),), -0.2, 0.2)), 0.3, 3.0),
    }


def reference(queries, keys, values, head_gain):
    factor = 1.0 / math.sqrt(HD)
    nblocks = TOKENS // WINDOW
    highest = lax.Precision.HIGHEST

    def blocked(matrix):
        return matrix.reshape(nblocks, WINDOW, HEADS, HD).transpose(0, 2, 1, 3)
    query_blocks = blocked(queries)
    key_blocks = blocked(keys)
    value_blocks = blocked(values)
    empty_block = jnp.zeros((1, HEADS, WINDOW, HD), jnp.float32)
    key_before = jnp.concatenate([empty_block, key_blocks[:-1]], axis=0)
    value_before = jnp.concatenate([empty_block, value_blocks[:-1]], axis=0)
    offsets = jnp.arange(WINDOW)
    causal = offsets[:, None] >= offsets[None, :]

    def advance(state, inputs):
        number, query_now, key_now, value_now, key_prev, value_prev = inputs
        key_both = jnp.concatenate([key_prev, key_now], axis=1)
        value_both = jnp.concatenate([value_prev, value_now], axis=1)
        scores = jnp.einsum('hqd,hkd->hqk', query_now, key_both, precision=highest) * factor
        query_pos = number * WINDOW + offsets
        key_pos = (number - 1) * WINDOW + jnp.arange(2 * WINDOW)
        spacing = query_pos[:, None] - key_pos[None, :]
        allowed = (spacing >= 0) & (spacing < WINDOW) & (key_pos >= 0)[None, :]
        scores = jnp.where(allowed[None], scores, -jnp.inf)
        biggest = lax.optimization_barrier(jnp.max(scores, axis=-1, keepdims=True))
        weights = jnp.exp(scores - biggest)
        window_out = jnp.einsum('hqk,hkd->hqd', weights, value_both, precision=highest) / lax.optimization_barrier(jnp.sum(weights, axis=-1, keepdims=True))
        inner_dot = jnp.einsum('hqd,hkd->hqk', query_now, key_now, precision=highest)
        inner_dot = jnp.where(causal[None], inner_dot, 0.0)
        linear_out = jnp.einsum('hqk,hkd->hqd', inner_dot, value_now, precision=highest)
        linear_out = linear_out + jnp.einsum('hqd,hde->hqe', query_now, state, precision=highest)
        state = state + jnp.einsum('hkd,hke->hde', key_now, value_now, precision=highest)
        return (state, (window_out, linear_out))
    start_state = jnp.zeros((HEADS, HD, HD), jnp.float32)
    numbers = jnp.arange(nblocks).astype(jnp.int32)
    final_state, outputs = lax.scan(advance, start_state, (numbers, query_blocks, key_blocks, value_blocks, key_before, value_before))
    window_all = outputs[0].transpose(0, 2, 1, 3).reshape(TOKENS, HEADS, HD)
    linear_all = outputs[1].transpose(0, 2, 1, 3).reshape(TOKENS, HEADS, HD)
    branch_a = window_all * head_gain[0][None, :, None]
    branch_b = linear_all * head_gain[1][None, :, None]
    norm_a = jnp.sqrt(lax.optimization_barrier(jnp.mean(branch_a * branch_a, axis=(1, 2))) + 1e-06)
    norm_b = jnp.sqrt(lax.optimization_barrier(jnp.mean(branch_b * branch_b, axis=(1, 2))) + 1e-06)
    mixed = branch_a / norm_a[:, None, None] + branch_b / norm_b[:, None, None]
    return mixed.reshape(TOKENS, HEADS * HD)
```

```python
import functools
import math

import jax
import jax.numpy as jnp
from jax import lax
from jax.experimental import pallas as pl
from jax.experimental.pallas import tpu as pltpu
from jax.sharding import PartitionSpec as P

HEADS = 64
HD = 128
WINDOW = 128
MESH = pl.DeviceIdType.MESH
F32 = jnp.float32
BF16 = jnp.bfloat16


def split(x):
    high = x.astype(BF16)
    low = (x - high.astype(F32)).astype(BF16)
    return high, low


def dot(a, b, ca, cb):
    return lax.dot_general(a, b, (((ca,), (cb,)), ((), ())), preferred_element_type=F32)


def wide(x):
    both = jnp.concatenate(split(x), axis=1)
    return jnp.concatenate([both, both], axis=0)


def kernel(
    ctx_count, head_axis, heads, rows,
    q_hbm, k_hbm, v_hbm, gain,
    out,
    kbuf, vbuf, qbuf, halo, k2, v2, q2, first, total, pair, chip, gather, prefix, piece_in, state, cross,
    a_buf, b_buf, acc_a, acc_b, zsend, zbuf,
    load_sem, halo_send, halo_recv, pair_send, pair_recv, gather_send, gather_recv,
    prefix_send, prefix_recv, cross_send, cross_recv, z_send, z_recv,
):
    ctx = lax.axis_index("ctx")
    z = lax.axis_index("head")
    core = lax.rem(ctx, 2)
    mine = lax.div(ctx, 2)
    chips = ctx_count // 2
    half = heads // 2
    per_head = chips // half
    depth = HD // per_head
    blocks = rows // HD
    factor = 1.0 / math.sqrt(HD)
    sibling = (ctx + 1 - 2 * core, z)
    following = (lax.rem(ctx + 1, ctx_count), z)
    preceding = (lax.rem(ctx + ctx_count - 1, ctx_count), z)
    side = 4 if chips == 16 else 0

    def owner(j, i):
        if side:
            return side * i + lax.rem(i + j, side)
        return j * per_head + i

    def piece_of(c):
        if side:
            y = lax.div(c, side)
            x = lax.rem(c, side)
            return side * lax.rem(x + side - y, side) + y
        return c

    def load(source, target, slot, h):
        columns = pl.ds(pl.multiple_of(h * HD, HD), HD)
        return pltpu.make_async_copy(source.at[:, columns], target.at[h], load_sem.at[slot, h])

    barrier = pltpu.get_barrier_semaphore()

    def greet(device):
        pl.semaphore_signal(barrier, inc=1, device_id=device, device_id_type=MESH)

    for jj in range(heads):
        h = lax.rem(jj + half * (1 - core), heads)
        load(k_hbm, kbuf, 0, h).start()
        load(v_hbm, vbuf, 1, h).start()
    greet(following)
    greet(preceding)
    greet(sibling)
    for d in range(1, chips):
        greet((2 * lax.rem(mine + d, chips) + core, z))
    for d in range(1, head_axis):
        greet((ctx, lax.rem(z + d, head_axis)))
    for h in range(heads):
        load(q_hbm, qbuf, 2, h).start()
    pl.semaphore_wait(barrier, 3 + chips - 1 + head_axis - 1)

    def halo_copy(slot):
        return pltpu.make_async_remote_copy(
            src_ref=(k_hbm, v_hbm)[slot].at[pl.ds(rows - HD, HD), :],
            dst_ref=halo.at[slot],
            send_sem=halo_send.at[slot],
            recv_sem=halo_recv.at[slot],
            device_id=following,
            device_id_type=MESH,
        )

    halo_copy(0).start()
    halo_copy(1).start()

    def local_state(h):
        load(k_hbm, kbuf, 0, h).wait()
        load(v_hbm, vbuf, 1, h).wait()
        k_high, k_low = split(kbuf[h])
        v_high, v_low = split(vbuf[h])
        k2[h, HD:, :HD] = k_high
        k2[h, HD:, HD:] = k_low
        v2[h, HD:, :HD] = v_high
        v2[h, HD:, HD:] = v_low
        kk = jnp.concatenate([k_high, k_low], axis=1)
        vv = jnp.concatenate([v_high, v_low], axis=1)
        mid = rows // 2
        parts = []
        for part in range(2):
            r = dot(kk[part * mid : (part + 1) * mid], vv[part * mid : (part + 1) * mid], 0, 0)
            parts.append(r[:HD, :HD] + (r[:HD, HD:] + r[HD:, :HD]))
        first[h] = parts[0]
        total[h] = parts[0] + parts[1]

    def pair_copy(j):
        return pltpu.make_async_remote_copy(
            src_ref=total.at[half * (1 - core) + j],
            dst_ref=pair.at[j],
            send_sem=pair_send.at[j],
            recv_sem=pair_recv.at[j],
            device_id=sibling,
            device_id_type=MESH,
        )

    def gather_copy(j, i, target, slot):
        return pltpu.make_async_remote_copy(
            src_ref=chip.at[j, pl.ds(i * depth, depth), :],
            dst_ref=gather.at[slot],
            send_sem=gather_send.at[j, i],
            recv_sem=gather_recv.at[slot],
            device_id=(2 * target + core, z),
            device_id_type=MESH,
        )

    @pl.loop(0, half)
    def _(j):
        local_state(half * (1 - core) + j)
        pair_copy(j).start()

    @pl.loop(0, half)
    def _(j):
        h = half * core + j
        local_state(h)
        pair_copy(j).wait_recv()
        chip[j] = total[h] + pair[j]
        for i in range(per_head):
            target = owner(j, i)

            @pl.when(target == mine)
            def _():
                gather[mine] = chip[j, i * depth : (i + 1) * depth, :]

            @pl.when(target != mine)
            def _():
                gather_copy(j, i, target, mine).start()

    row = lax.broadcasted_iota(jnp.int32, (HD, 2 * HD), 0)
    col = lax.broadcasted_iota(jnp.int32, (HD, 2 * HD), 1)
    band = (col > row) & (col <= row + HD)
    causal_even = (col >= HD) & (col <= row + HD)
    causal_odd = col <= row + HD

    acc_a[...] = jnp.zeros_like(acc_a)
    acc_b[...] = jnp.zeros_like(acc_b)

    def block(h, n, allowed, causal):
        here = slice(n * HD, (n + 1) * HD)
        both = slice(n * HD, (n + 2) * HD)
        q_low_high = q2[h, here, :]
        k_pair = k2[h, both, :]
        s = dot(q_low_high[:, HD:], k_pair[:, :HD], 1, 1) + dot(q_low_high, k_pair, 1, 1)
        masked = jnp.where(allowed, s, -jnp.inf)
        biggest = jnp.max(masked, axis=1, keepdims=True)
        weights = jnp.exp((masked - biggest) * factor)
        weight_sum = jnp.sum(weights, axis=1, keepdims=True)
        inner = jnp.where(causal, s, 0.0)
        stacked = jnp.concatenate(split(weights) + split(inner), axis=0)
        r = dot(stacked, v2[h, both, :], 1, 0)
        win = r[:HD, :HD] + (r[:HD, HD:] + r[HD : 2 * HD, :HD])
        lin = r[2 * HD : 3 * HD, :HD] + (r[2 * HD : 3 * HD, HD:] + r[3 * HD :, :HD])
        a = win * (gain[0, h] / weight_sum)
        a_buf[h, here, :] = a
        acc_a[here, :] += a * a
        return lin

    def inner_blocks(h):
        load(q_hbm, qbuf, 2, h).wait()
        q_high, q_low = split(qbuf[h])
        q2[h, :, :HD] = q_low
        q2[h, :, HD:] = q_high
        mid = rows // 2
        carried = dot(q2[h, mid:, :], wide(first[h]), 1, 0)
        carried = carried[:, :HD] + carried[:, HD:]
        for n in range(1, blocks):
            lin = block(h, n, band, causal_odd if n % 2 else causal_even)
            if n * HD >= mid:
                lin = lin + carried[n * HD - mid : (n + 1) * HD - mid]
            b_buf[h, n * HD : (n + 1) * HD, :] = lin

    cut = heads // 2

    @pl.loop(0, cut)
    def _(h):
        inner_blocks(h)

    def prefix_copy(d, slot):
        target = lax.rem(mine + d, chips)
        return pltpu.make_async_remote_copy(
            src_ref=prefix.at[target],
            dst_ref=piece_in.at[slot],
            send_sem=prefix_send.at[d],
            recv_sem=prefix_recv.at[slot],
            device_id=(2 * target + core, z),
            device_id_type=MESH,
        )

    @pl.loop(1, chips)
    def _(d):
        gather_copy(0, 0, mine, lax.rem(mine + d, chips)).wait_recv()

    running = jnp.zeros((depth, HD), F32)
    for c in range(chips):
        prefix[c] = running
        if c < chips - 1:
            running = running + gather[c]
    my_piece = piece_of(mine)
    piece_in[my_piece] = prefix[mine]

    @pl.loop(1, chips)
    def _(d):
        prefix_copy(d, my_piece).start()

    @pl.loop(cut, heads)
    def _(h):
        inner_blocks(h)

    def cross_copy(j):
        return pltpu.make_async_remote_copy(
            src_ref=cross.at[j],
            dst_ref=state.at[half * core + j],
            send_sem=cross_send.at[j],
            recv_sem=cross_recv.at[j],
            device_id=sibling,
            device_id_type=MESH,
        )

    @pl.loop(0, half)
    def _(j):
        h = half * core + j
        for i in range(per_head):
            p = j * per_head + i

            @pl.when(p != my_piece)
            def _():
                prefix_copy(1, p).wait_recv()

        before = piece_in[pl.ds(j * per_head, per_head)].reshape(HD, HD)
        state[h] = before + jnp.where(core == 1, pair[j], 0.0)
        cross[j] = before + jnp.where(core == 0, total[h], 0.0)
        cross_copy(j).start()

    halo_copy(0).wait_recv()
    halo_copy(1).wait_recv()
    band_first = band & ((col >= HD) | (ctx > 0))

    @pl.loop(0, heads)
    def _(h):
        columns = pl.ds(pl.multiple_of(h * HD, HD), HD)
        k_high, k_low = split(halo[0, :, columns])
        v_high, v_low = split(halo[1, :, columns])
        k2[h, :HD, :HD] = k_high
        k2[h, :HD, HD:] = k_low
        v2[h, :HD, :HD] = v_high
        v2[h, :HD, HD:] = v_low
        b_buf[h, :HD, :] = block(h, 0, band_first, causal_even)

    def last_linear(h):
        r = dot(q2[h], wide(state[h]), 1, 0)
        b = (b_buf[h] + (r[:, :HD] + r[:, HD:])) * gain[1, h]
        b_buf[h] = b
        acc_b[...] += b * b

    @pl.loop(0, half)
    def _(j):
        last_linear(half * core + j)

    @pl.loop(0, half)
    def _(j):
        cross_copy(j).wait_recv()
        last_linear(half * (1 - core) + j)

    sums = []
    for acc in (acc_a, acc_b):
        for n in range(blocks):
            turned = jnp.transpose(acc[n * HD : (n + 1) * HD, :])
            sums.append(jnp.sum(turned, axis=0, keepdims=True))
    sums = jnp.concatenate(sums, axis=0)
    zsend[...] = sums
    zbuf[z] = sums

    def z_copy(d, slot):
        return pltpu.make_async_remote_copy(
            src_ref=zsend,
            dst_ref=zbuf.at[slot],
            send_sem=z_send.at[d],
            recv_sem=z_recv.at[slot],
            device_id=(ctx, lax.rem(z + d, head_axis)),
            device_id_type=MESH,
        )

    for d in range(1, head_axis):
        z_copy(d, z).start()
    for d in range(1, head_axis):
        z_copy(d, lax.rem(z + d, head_axis)).wait_recv()
    squares = zbuf[0]
    for other in range(1, head_axis):
        squares = squares + zbuf[other]
    inverse = 1.0 / jnp.sqrt(squares / (heads * head_axis * HD) + 1e-06)
    inverse = jnp.concatenate([inverse, jnp.zeros((HD - 2 * blocks, HD), F32)], axis=0)
    columns = jnp.transpose(inverse)
    for n in range(blocks):
        here = slice(n * HD, (n + 1) * HD)
        scale_a = columns[:, n : n + 1]
        scale_b = columns[:, blocks + n : blocks + n + 1]
        for h in range(heads):
            out[here, h * HD : (h + 1) * HD] = a_buf[h, here, :] * scale_a + b_buf[h, here, :] * scale_b

    for slot in range(2):
        halo_copy(slot).wait_send()
    for d in range(1, head_axis):
        z_copy(d, z).wait_send()

    @pl.loop(0, half)
    def _(j):
        pair_copy(j).wait_send()
        cross_copy(j).wait_send()
        for i in range(per_head):
            @pl.when(owner(j, i) != mine)
            def _():
                gather_copy(j, i, owner(j, i), mine).wait_send()

    @pl.loop(1, chips)
    def _(d):
        prefix_copy(d, my_piece).wait_send()


def shards(ctx_count, head_axis, queries, keys, values, head_gain):
    rows = queries.shape[0]
    heads = head_gain.shape[1]
    chips = ctx_count // 2
    half = heads // 2
    depth = half * HD // chips
    per_head = chips // half
    blocks = rows // HD
    anywhere = pl.BlockSpec(memory_space=pl.ANY)
    dma = pltpu.SemaphoreType.DMA
    vmem = pltpu.VMEM
    body = functools.partial(kernel, ctx_count, head_axis, heads, rows)
    return pl.pallas_call(
        body,
        out_shape=jax.ShapeDtypeStruct((rows, heads * HD), F32),
        in_specs=[anywhere, anywhere, anywhere, pl.BlockSpec(memory_space=pltpu.SMEM)],
        out_specs=pl.BlockSpec(memory_space=pltpu.VMEM),
        scratch_shapes=[
            vmem((heads, rows, HD), F32),
            vmem((heads, rows, HD), F32),
            vmem((heads, rows, HD), F32),
            vmem((2, HD, heads * HD), F32),
            vmem((heads, rows + HD, 2 * HD), BF16),
            vmem((heads, rows + HD, 2 * HD), BF16),
            vmem((heads, rows, 2 * HD), BF16),
            vmem((heads, HD, HD), F32),
            vmem((heads, HD, HD), F32),
            vmem((half, HD, HD), F32),
            vmem((half, HD, HD), F32),
            vmem((chips, depth, HD), F32),
            vmem((chips, depth, HD), F32),
            vmem((chips, depth, HD), F32),
            vmem((heads, HD, HD), F32),
            vmem((half, HD, HD), F32),
            vmem((heads, rows, HD), F32),
            vmem((heads, rows, HD), F32),
            vmem((rows, HD), F32),
            vmem((rows, HD), F32),
            vmem((2 * blocks, HD), F32),
            vmem((head_axis, 2 * blocks, HD), F32),
            dma((3, heads)),
            dma((2,)),
            dma((2,)),
            dma((half,)),
            dma((half,)),
            dma((half, per_head)),
            dma((chips,)),
            dma((chips,)),
            dma((chips,)),
            dma((half,)),
            dma((half,)),
            dma((head_axis,)),
            dma((head_axis,)),
        ],
        compiler_params=pltpu.CompilerParams(
            collective_id=0, has_side_effects=True, vmem_limit_bytes=60 * 1024 * 1024
        ),
    )(queries, keys, values, head_gain)


def solution(mesh):
    body = functools.partial(shards, mesh.shape["ctx"], mesh.shape["head"])
    in_specs = (P("ctx", "head"), P("ctx", "head"), P("ctx", "head"), P(None, "head"))
    return jax.shard_map(body, mesh=mesh, in_specs=in_specs, out_specs=P("ctx", "head"), check_vma=False)
```

```python
import functools
import math

import jax
import jax.numpy as jnp
from jax import lax
from jax.experimental import pallas as pl
from jax.experimental.pallas import tpu as pltpu
from jax.sharding import PartitionSpec as P

HEADS = 64
HD = 128
WINDOW = 128
MESH = pl.DeviceIdType.MESH
F32 = jnp.float32
BF16 = jnp.bfloat16


def split(x):
    high = x.astype(BF16)
    low = (x - high.astype(F32)).astype(BF16)
    return high, low


def dot(a, b, ca, cb):
    return lax.dot_general(a, b, (((ca,), (cb,)), ((), ())), preferred_element_type=F32)


def wide(x):
    both = jnp.concatenate(split(x), axis=1)
    return jnp.concatenate([both, both], axis=0)


def kernel(
    ctx_count, head_axis, heads, rows,
    q_hbm, k_hbm, v_hbm, gain,
    out,
    kbuf, vbuf, qbuf, asked, answer, answered, told, heard, own_peak, own_sum, k2, v2, q2, first, total, pair, chip, gather, prefix, piece_in, state, cross,
    a_buf, b_buf, acc_a, acc_b, zsend, zbuf,
    load_sem, ask_send, ask_recv, answer_send, answer_recv, told_send, told_recv, pair_send, pair_recv, gather_send, gather_recv,
    prefix_send, prefix_recv, cross_send, cross_recv, z_send, z_recv,
):
    ctx = lax.axis_index("ctx")
    z = lax.axis_index("head")
    core = lax.rem(ctx, 2)
    mine = lax.div(ctx, 2)
    chips = ctx_count // 2
    half = heads // 2
    per_head = chips // half
    depth = HD // per_head
    blocks = rows // HD
    factor = 1.0 / math.sqrt(HD)
    sibling = (ctx + 1 - 2 * core, z)
    following = (lax.rem(ctx + 1, ctx_count), z)
    preceding = (lax.rem(ctx + ctx_count - 1, ctx_count), z)
    side = 4 if chips == 16 else 0

    def owner(j, i):
        if side:
            return side * i + lax.rem(i + j, side)
        return j * per_head + i

    def piece_of(c):
        if side:
            y = lax.div(c, side)
            x = lax.rem(c, side)
            return side * lax.rem(x + side - y, side) + y
        return c

    def load(source, target, slot, h):
        columns = pl.ds(pl.multiple_of(h * HD, HD), HD)
        return pltpu.make_async_copy(source.at[:, columns], target.at[h], load_sem.at[slot, h])

    sent = []

    barrier = pltpu.get_barrier_semaphore()

    def greet(device):
        pl.semaphore_signal(barrier, inc=1, device_id=device, device_id_type=MESH)

    for jj in range(heads):
        h = lax.rem(jj + half * (1 - core), heads)
        load(k_hbm, kbuf, 0, h).start()
        load(v_hbm, vbuf, 1, h).start()
    greet(following)
    greet(preceding)
    greet(sibling)
    for d in range(1, chips):
        greet((2 * lax.rem(mine + d, chips) + core, z))
    for d in range(1, head_axis):
        greet((ctx, lax.rem(z + d, head_axis)))
    for h in range(heads):
        load(q_hbm, qbuf, 2, h).start()
    groups = heads // 2
    last = slice(rows - HD, rows)

    def ask_copy(g):
        return pltpu.make_async_remote_copy(
            src_ref=q_hbm.at[pl.ds(0, HD), pl.ds(pl.multiple_of(g * 2 * HD, HD), 2 * HD)],
            dst_ref=asked.at[g],
            send_sem=ask_send.at[g],
            recv_sem=ask_recv.at[g],
            device_id=preceding,
            device_id_type=MESH,
        )

    def answer_copy(g):
        return pltpu.make_async_remote_copy(
            src_ref=answer.at[g],
            dst_ref=answered.at[g],
            send_sem=answer_send.at[g],
            recv_sem=answer_recv.at[g],
            device_id=following,
            device_id_type=MESH,
        )

    def told_copy():
        return pltpu.make_async_remote_copy(
            src_ref=told,
            dst_ref=heard,
            send_sem=told_send,
            recv_sem=told_recv,
            device_id=following,
            device_id_type=MESH,
        )

    def local_state(h):
        load(k_hbm, kbuf, 0, h).wait()
        load(v_hbm, vbuf, 1, h).wait()
        k_high, k_low = split(kbuf[h])
        v_high, v_low = split(vbuf[h])
        k2[h, :, :HD] = k_high
        k2[h, :, HD:] = k_low
        v2[h, :, :HD] = v_high
        v2[h, :, HD:] = v_low
        kk = jnp.concatenate([k_high, k_low], axis=1)
        vv = jnp.concatenate([v_high, v_low], axis=1)
        mid = rows // 2
        parts = []
        for part in range(2):
            r = dot(kk[part * mid : (part + 1) * mid], vv[part * mid : (part + 1) * mid], 0, 0)
            parts.append(r[:HD, :HD] + (r[:HD, HD:] + r[HD:, :HD]))
        first[h] = parts[0]
        total[h] = parts[0] + parts[1]

    def pair_copy(j):
        return pltpu.make_async_remote_copy(
            src_ref=total.at[half * (1 - core) + j],
            dst_ref=pair.at[j],
            send_sem=pair_send.at[j],
            recv_sem=pair_recv.at[j],
            device_id=sibling,
            device_id_type=MESH,
        )

    def gather_copy(j, i, target, slot):
        return pltpu.make_async_remote_copy(
            src_ref=chip.at[j, pl.ds(i * depth, depth), :],
            dst_ref=gather.at[slot],
            send_sem=gather_send.at[j, i],
            recv_sem=gather_recv.at[slot],
            device_id=(2 * target + core, z),
            device_id_type=MESH,
        )

    @pl.loop(0, half)
    def _(j):
        local_state(half * (1 - core) + j)

    pl.semaphore_wait(barrier, 3 + chips - 1 + head_axis - 1)
    for j in range(half):
        pair_copy(j).start()
    for g in range(groups):
        ask_copy(g).start()
        sent.append(ask_copy(g).wait_send)

    def pair_done():
        @pl.loop(0, half)
        def _(j):
            pair_copy(j).wait_send()

    sent.append(pair_done)

    @pl.loop(0, half)
    def _(j):
        h = half * core + j
        local_state(h)
        pair_copy(j).wait_recv()
        chip[j] = total[h] + pair[j]
        for i in range(per_head):
            target = owner(j, i)

            @pl.when(target == mine)
            def _():
                gather[mine] = chip[j, i * depth : (i + 1) * depth, :]

            @pl.when(target != mine)
            def _():
                gather_copy(j, i, target, mine).start()

    def gather_done():
        @pl.loop(0, half)
        def _(j):
            for i in range(per_head):
                @pl.when(owner(j, i) != mine)
                def _():
                    gather_copy(j, i, owner(j, i), mine).wait_send()

    sent.append(gather_done)

    row = lax.broadcasted_iota(jnp.int32, (HD, 2 * HD), 0)
    col = lax.broadcasted_iota(jnp.int32, (HD, 2 * HD), 1)
    band = (col > row) & (col <= row + HD)
    causal_even = (col >= HD) & (col <= row + HD)
    causal_odd = col <= row + HD
    lane = col[:, :HD]
    lower = lane <= row[:, :HD]

    acc_a[...] = jnp.zeros_like(acc_a)
    acc_b[...] = jnp.zeros_like(acc_b)
    told[...] = jnp.zeros_like(told)
    own_peak[...] = jnp.zeros_like(own_peak)
    own_sum[...] = jnp.zeros_like(own_sum)

    def scores(q_low_high, keys):
        return dot(q_low_high[:, HD:], keys[:, :HD], 1, 1) + dot(q_low_high, keys, 1, 1)

    def block(h, n):
        here = slice(n * HD, (n + 1) * HD)
        both = slice(max(n - 1, 0) * HD, (n + 1) * HD)
        allowed = band if n else lower
        causal = (causal_odd if n % 2 else causal_even) if n else lower
        s = scores(q2[h, here, :], k2[h, both, :])
        masked = jnp.where(allowed, s, -jnp.inf)
        biggest = jnp.max(masked, axis=1, keepdims=True)
        weights = jnp.exp((masked - biggest) * factor)
        weight_sum = jnp.sum(weights, axis=1, keepdims=True)
        inner = jnp.where(causal, s, 0.0)
        stacked = jnp.concatenate(split(weights) + split(inner), axis=0)
        r = dot(stacked, v2[h, both, :], 1, 0)
        win = r[:HD, :HD] + (r[:HD, HD:] + r[HD : 2 * HD, :HD])
        lin = r[2 * HD : 3 * HD, :HD] + (r[2 * HD : 3 * HD, HD:] + r[3 * HD :, :HD])
        if n:
            a = win * (gain[0, h] / weight_sum)
            a_buf[h, here, :] = a
            acc_a[here, :] += a * a
        else:
            a_buf[h, here, :] = win
            own_peak[...] = jnp.where(lane == h, biggest, own_peak[...])
            own_sum[...] = jnp.where(lane == h, weight_sum, own_sum[...])
        return lin

    def inner_blocks(h):
        load(q_hbm, qbuf, 2, h).wait()
        q_high, q_low = split(qbuf[h])
        q2[h, :, :HD] = q_low
        q2[h, :, HD:] = q_high
        mid = rows // 2
        carried = dot(q2[h, mid:, :], wide(first[h]), 1, 0)
        carried = carried[:, :HD] + carried[:, HD:]
        for n in range(blocks):
            lin = block(h, n)
            if n * HD >= mid:
                lin = lin + carried[n * HD - mid : (n + 1) * HD - mid]
            b_buf[h, n * HD : (n + 1) * HD, :] = lin

    def answer_group(g):
        ask_copy(g).wait_recv()
        for e in range(2):
            h = 2 * g + e
            columns = slice(e * HD, (e + 1) * HD)
            q_high, q_low = split(asked[g, :, columns])
            s = scores(jnp.concatenate([q_low, q_high], axis=1), k2[h, last, :])
            biggest = jnp.max(jnp.where(lower, -3e38, s), axis=1, keepdims=True)
            weights = jnp.where(lower, 0.0, jnp.exp((s - biggest) * factor))
            weight_sum = jnp.sum(weights, axis=1, keepdims=True)
            r = dot(jnp.concatenate(split(weights), axis=0), v2[h, last, :], 1, 0)
            answer[g, :, columns] = r[:HD, :HD] + (r[:HD, HD:] + r[HD:, :HD])
            told[...] = jnp.where(
                lane == h, biggest, jnp.where(lane == heads + h, weight_sum, told[...])
            )
        answer_copy(g).start()

    early = heads - groups - 2

    @pl.loop(0, early)
    def _(h):
        inner_blocks(h)

    @pl.loop(0, groups)
    def _(g):
        answer_group(g)
        inner_blocks(early + g)

    def answer_done():
        @pl.loop(0, groups)
        def _(g):
            answer_copy(g).wait_send()

        told_copy().wait_send()

    told_copy().start()
    sent.append(answer_done)

    def prefix_copy(d, slot):
        target = lax.rem(mine + d, chips)
        return pltpu.make_async_remote_copy(
            src_ref=prefix.at[target],
            dst_ref=piece_in.at[slot],
            send_sem=prefix_send.at[d],
            recv_sem=prefix_recv.at[slot],
            device_id=(2 * target + core, z),
            device_id_type=MESH,
        )

    @pl.loop(1, chips)
    def _(d):
        gather_copy(0, 0, mine, lax.rem(mine + d, chips)).wait_recv()

    running = jnp.zeros((depth, HD), F32)
    for c in range(chips):
        prefix[c] = running
        if c < chips - 1:
            running = running + gather[c]
    my_piece = piece_of(mine)
    piece_in[my_piece] = prefix[mine]

    @pl.loop(1, chips)
    def _(d):
        prefix_copy(d, my_piece).start()

    def prefix_done():
        @pl.loop(1, chips)
        def _(d):
            prefix_copy(d, my_piece).wait_send()

    sent.append(prefix_done)

    @pl.loop(early + groups, heads)
    def _(h):
        inner_blocks(h)

    def cross_copy(j):
        return pltpu.make_async_remote_copy(
            src_ref=cross.at[j],
            dst_ref=state.at[half * core + j],
            send_sem=cross_send.at[j],
            recv_sem=cross_recv.at[j],
            device_id=sibling,
            device_id_type=MESH,
        )

    @pl.loop(0, half)
    def _(j):
        h = half * core + j
        for i in range(per_head):
            p = j * per_head + i

            @pl.when(p != my_piece)
            def _():
                prefix_copy(1, p).wait_recv()

        before = piece_in[pl.ds(j * per_head, per_head)].reshape(HD, HD)
        state[h] = before + jnp.where(core == 1, pair[j], 0.0)
        cross[j] = before + jnp.where(core == 0, total[h], 0.0)
        cross_copy(j).start()

    def cross_done():
        @pl.loop(0, half)
        def _(j):
            cross_copy(j).wait_send()

    sent.append(cross_done)

    def merge():
        for g in range(groups):
            answer_copy(g).wait_recv()
        told_copy().wait_recv()
        peak = own_peak[...]
        other_peak = jnp.where(ctx > 0, heard[...], -3e38)
        other_sum = pltpu.roll(heard[...], HD - heads, 1)
        biggest = jnp.maximum(peak, other_peak)
        scale = jnp.exp((peak - biggest) * factor)
        other_scale = jnp.where(ctx > 0, jnp.exp((other_peak - biggest) * factor), 0.0)
        whole = own_sum[...] * scale + other_sum * other_scale
        scale = scale / whole
        other_scale = other_scale / whole
        square = acc_a[:HD, :]
        for h in range(heads):
            columns = slice(h % 2 * HD, (h % 2 + 1) * HD)
            a = a_buf[h, :HD, :] * scale[:, h : h + 1]
            a = (a + answered[h // 2, :, columns] * other_scale[:, h : h + 1]) * gain[0, h]
            a_buf[h, :HD, :] = a
            square = square + a * a
        acc_a[:HD, :] = square

    def last_linear(h):
        r = dot(q2[h], wide(state[h]), 1, 0)
        b = (b_buf[h] + (r[:, :HD] + r[:, HD:])) * gain[1, h]
        b_buf[h] = b
        acc_b[...] += b * b

    @pl.loop(0, half)
    def _(j):
        last_linear(half * core + j)

    @pl.loop(0, half)
    def _(j):
        cross_copy(j).wait_recv()
        last_linear(half * (1 - core) + j)

    merge()

    sums = []
    for acc in (acc_a, acc_b):
        for n in range(blocks):
            turned = jnp.transpose(acc[n * HD : (n + 1) * HD, :])
            sums.append(jnp.sum(turned, axis=0, keepdims=True))
    sums = jnp.concatenate(sums, axis=0)
    zsend[...] = sums
    zbuf[z] = sums

    def z_copy(d, slot):
        return pltpu.make_async_remote_copy(
            src_ref=zsend,
            dst_ref=zbuf.at[slot],
            send_sem=z_send.at[d],
            recv_sem=z_recv.at[slot],
            device_id=(ctx, lax.rem(z + d, head_axis)),
            device_id_type=MESH,
        )

    for d in range(1, head_axis):
        z_copy(d, z).start()
        sent.append(z_copy(d, z).wait_send)
    for d in range(1, head_axis):
        z_copy(d, lax.rem(z + d, head_axis)).wait_recv()
    squares = zbuf[0]
    for other in range(1, head_axis):
        squares = squares + zbuf[other]
    inverse = 1.0 / jnp.sqrt(squares / (heads * head_axis * HD) + 1e-06)
    inverse = jnp.concatenate([inverse, jnp.zeros((HD - 2 * blocks, HD), F32)], axis=0)
    columns = jnp.transpose(inverse)
    for n in range(blocks):
        here = slice(n * HD, (n + 1) * HD)
        scale_a = columns[:, n : n + 1]
        scale_b = columns[:, blocks + n : blocks + n + 1]
        for h in range(heads):
            out[here, h * HD : (h + 1) * HD] = a_buf[h, here, :] * scale_a + b_buf[h, here, :] * scale_b

    for finish in sent:
        finish()


def shards(ctx_count, head_axis, queries, keys, values, head_gain):
    rows = queries.shape[0]
    heads = head_gain.shape[1]
    chips = ctx_count // 2
    half = heads // 2
    depth = half * HD // chips
    per_head = chips // half
    blocks = rows // HD
    anywhere = pl.BlockSpec(memory_space=pl.ANY)
    dma = pltpu.SemaphoreType.DMA
    vmem = pltpu.VMEM
    body = functools.partial(kernel, ctx_count, head_axis, heads, rows)
    return pl.pallas_call(
        body,
        out_shape=pltpu.VMEM((rows, heads * HD), F32),
        in_specs=[anywhere, anywhere, anywhere, pl.BlockSpec(memory_space=pltpu.SMEM)],
        out_specs=pl.BlockSpec(memory_space=pltpu.VMEM),
        scratch_shapes=[
            vmem((heads, rows, HD), F32),
            vmem((heads, rows, HD), F32),
            vmem((heads, rows, HD), F32),
            vmem((heads // 2, HD, 2 * HD), F32),
            vmem((heads // 2, HD, 2 * HD), F32),
            vmem((heads // 2, HD, 2 * HD), F32),
            vmem((HD, HD), F32),
            vmem((HD, HD), F32),
            vmem((HD, HD), F32),
            vmem((HD, HD), F32),
            vmem((heads, rows, 2 * HD), BF16),
            vmem((heads, rows, 2 * HD), BF16),
            vmem((heads, rows, 2 * HD), BF16),
            vmem((heads, HD, HD), F32),
            vmem((heads, HD, HD), F32),
            vmem((half, HD, HD), F32),
            vmem((half, HD, HD), F32),
            vmem((chips, depth, HD), F32),
            vmem((chips, depth, HD), F32),
            vmem((chips, depth, HD), F32),
            vmem((heads, HD, HD), F32),
            vmem((half, HD, HD), F32),
            vmem((heads, rows, HD), F32),
            vmem((heads, rows, HD), F32),
            vmem((rows, HD), F32),
            vmem((rows, HD), F32),
            vmem((2 * blocks, HD), F32),
            vmem((head_axis, 2 * blocks, HD), F32),
            dma((3, heads)),
            dma((heads // 2,)),
            dma((heads // 2,)),
            dma((heads // 2,)),
            dma((heads // 2,)),
            dma,
            dma,
            dma((half,)),
            dma((half,)),
            dma((half, per_head)),
            dma((chips,)),
            dma((chips,)),
            dma((chips,)),
            dma((half,)),
            dma((half,)),
            dma((head_axis,)),
            dma((head_axis,)),
        ],
        compiler_params=pltpu.CompilerParams(
            collective_id=0, has_side_effects=True, vmem_limit_bytes=60 * 1024 * 1024
        ),
    )(queries, keys, values, head_gain)


def solution(mesh):
    body = functools.partial(shards, mesh.shape["ctx"], mesh.shape["head"])
    in_specs = (P("ctx", "head"), P("ctx", "head"), P("ctx", "head"), P(None, "head"))
    return jax.shard_map(body, mesh=mesh, in_specs=in_specs, out_specs=P("ctx", "head"), check_vma=False)
```

```python
import functools
import math

import jax
import jax.numpy as jnp
from jax import lax
from jax.experimental import pallas as pl
from jax.experimental.pallas import tpu as pltpu
from jax.sharding import PartitionSpec as P

HEADS = 64
HD = 128
WINDOW = 128
MESH = pl.DeviceIdType.MESH
PARTS = 2
START = (("v", 0), ("q", 0), ("q", 1),)
ORDER = (("q", 2), ("i", 0), ("i", 1), ("i", 2), ("i", 3), ("a", 0), ("p", 0), ("a", 1), ("i", 4), ("p", 1), ("i", 5), ("i", 6), ("a", 2), ("i", 7), ("k", 0), ("f", 0), ("f", 1), ("f", 2), ("f", 3),)
F32 = jnp.float32
BF16 = jnp.bfloat16


def split(x):
    high = x.astype(BF16)
    low = (x - high.astype(F32)).astype(BF16)
    return high, low


def dot(a, b, ca, cb):
    return lax.dot_general(a, b, (((ca,), (cb,)), ((), ())), preferred_element_type=F32)


def wide(x):
    both = jnp.concatenate(split(x), axis=1)
    return jnp.concatenate([both, both], axis=0)


def kernel(
    ctx_count, head_axis, heads, rows,
    q_hbm, k_hbm, v_hbm, gain,
    out,
    kbuf, vbuf, qbuf, asked, answer, answered, halo, told, heard, kept, own_peak, own_sum, k2, v2, q2, first, total, pair, chip, gather, prefix, piece_in, state, cross,
    a_buf, b_buf, acc_a, acc_b, zsend, zbuf,
    load_sem, halo_send, halo_recv, ask_send, ask_recv, answer_send, answer_recv, told_send, told_recv, pair_send, pair_recv, gather_send, gather_recv,
    prefix_send, prefix_recv, cross_send, cross_recv, z_send, z_recv,
):
    ctx = lax.axis_index("ctx")
    z = lax.axis_index("head")
    core = lax.rem(ctx, 2)
    mine = lax.div(ctx, 2)
    chips = ctx_count // 2
    half = heads // 2
    each = half // PARTS
    depth = each * HD // chips
    blocks = rows // HD
    factor = 1.0 / math.sqrt(HD)
    sibling = (ctx + 1 - 2 * core, z)
    following = (lax.rem(ctx + 1, ctx_count), z)
    preceding = (lax.rem(ctx + ctx_count - 1, ctx_count), z)
    side = math.isqrt(chips)
    my_y, my_x = lax.div(mine, side), lax.rem(mine, side)
    others = []
    for dy in range(side):
        for dx in range(side):
            hops = min(dx, side - dx) + min(dy, side - dy)
            if hops:
                other = lax.rem(my_y + dy, side) * side + lax.rem(my_x + dx, side)
                others.append((hops, len(others), other))
    others = [other for _, _, other in sorted(others, key=lambda o: (-o[0], o[1]))]

    def piece(c):
        return pl.ds(pl.multiple_of(c * depth, depth), depth)

    def load(source, target, slot, h):
        columns = pl.ds(pl.multiple_of(h * HD, HD), HD)
        return pltpu.make_async_copy(source.at[:, columns], target.at[h], load_sem.at[slot, h])

    sent = []

    barrier = pltpu.get_barrier_semaphore()

    def greet(device):
        pl.semaphore_signal(barrier, inc=1, device_id=device, device_id_type=MESH)

    for jj in range(heads):
        h = lax.rem(jj + half * (1 - core), heads)
        load(k_hbm, kbuf, 0, h).start()
        load(v_hbm, vbuf, 1, h).start()
    greet(following)
    greet(preceding)
    greet(sibling)
    for other in others:
        greet((2 * other + core, z))
    for d in range(1, head_axis):
        greet((ctx, lax.rem(z + d, head_axis)))
    for h in range(heads):
        load(q_hbm, qbuf, 2, h).start()
    groups = heads // 2 - 1
    last = slice(rows - HD, rows)

    def ask_copy(g):
        return pltpu.make_async_remote_copy(
            src_ref=q_hbm.at[pl.ds(0, HD), pl.ds(pl.multiple_of(g * 2 * HD, HD), 2 * HD)],
            dst_ref=asked.at[g],
            send_sem=ask_send.at[g],
            recv_sem=ask_recv.at[g],
            device_id=preceding,
            device_id_type=MESH,
        )

    def answer_copy(g):
        return pltpu.make_async_remote_copy(
            src_ref=answer.at[g],
            dst_ref=answered.at[g],
            send_sem=answer_send.at[g],
            recv_sem=answer_recv.at[g],
            device_id=following,
            device_id_type=MESH,
        )

    kept_columns = pl.ds(groups * 2 * HD, 2 * HD)

    def halo_copy(slot):
        return pltpu.make_async_remote_copy(
            src_ref=(k_hbm, v_hbm)[slot].at[pl.ds(rows - HD, HD), kept_columns],
            dst_ref=halo.at[slot],
            send_sem=halo_send.at[slot],
            recv_sem=halo_recv.at[slot],
            device_id=following,
            device_id_type=MESH,
        )

    def send_halo(_):
        for slot in range(2):
            halo_copy(slot).start()

    def ask(g):
        ask_copy(g).start()

    def told_copy():
        return pltpu.make_async_remote_copy(
            src_ref=told,
            dst_ref=heard,
            send_sem=told_send,
            recv_sem=told_recv,
            device_id=following,
            device_id_type=MESH,
        )

    def local_state(h):
        load(k_hbm, kbuf, 0, h).wait()
        load(v_hbm, vbuf, 1, h).wait()
        k_high, k_low = split(kbuf[h])
        v_high, v_low = split(vbuf[h])
        k2[h, :, :HD] = k_high
        k2[h, :, HD:] = k_low
        v2[h, :, :HD] = v_high
        v2[h, :, HD:] = v_low
        kk = jnp.concatenate([k_high, k_low], axis=1)
        vv = jnp.concatenate([v_high, v_low], axis=1)
        mid = rows // 2
        parts = []
        for part in range(2):
            r = dot(kk[part * mid : (part + 1) * mid], vv[part * mid : (part + 1) * mid], 0, 0)
            parts.append(r[:HD, :HD] + (r[:HD, HD:] + r[HD:, :HD]))
        first[h] = parts[0]
        total[h] = parts[0] + parts[1]

    def pair_copy(j):
        return pltpu.make_async_remote_copy(
            src_ref=total.at[half * (1 - core) + j],
            dst_ref=pair.at[j],
            send_sem=pair_send.at[j],
            recv_sem=pair_recv.at[j],
            device_id=sibling,
            device_id_type=MESH,
        )

    def gather_copy(j, target):
        return pltpu.make_async_remote_copy(
            src_ref=chip.at[j, piece(target), :],
            dst_ref=gather.at[j, mine],
            send_sem=gather_send.at[j],
            recv_sem=gather_recv.at[j],
            device_id=(2 * target + core, z),
            device_id_type=MESH,
        )

    def prefix_copy(j, target):
        return pltpu.make_async_remote_copy(
            src_ref=prefix.at[j, target],
            dst_ref=piece_in.at[j, piece(mine), :],
            send_sem=prefix_send.at[j],
            recv_sem=prefix_recv.at[j],
            device_id=(2 * target + core, z),
            device_id_type=MESH,
        )

    def all_others(semaphore):
        sample = gather.at[0, pl.ds(0, chips - 1)]
        pltpu.make_async_copy(sample, sample, semaphore).wait()

    @pl.loop(0, half)
    def _(j):
        local_state(half * (1 - core) + j)

    pl.semaphore_wait(barrier, 3 + chips - 1 + head_axis - 1)
    for j in range(half):
        pair_copy(j).start()
    for name, which in START:
        {"v": send_halo, "q": ask}[name](which)
    for g in range(groups):
        sent.append(ask_copy(g).wait_send)
    for slot in range(2):
        sent.append(halo_copy(slot).wait_send)

    def pair_done():
        @pl.loop(0, half)
        def _(j):
            pair_copy(j).wait_send()

    sent.append(pair_done)

    @pl.loop(0, PARTS)
    def _(p):
        for e in range(each):
            j = p * each + e
            h = half * core + j
            local_state(h)
            pair_copy(j).wait_recv()
            chip[p, e * HD : (e + 1) * HD, :] = total[h] + pair[j]
        gather[p, mine] = chip[p, piece(mine), :]
        for other in others:
            gather_copy(p, other).start()

    def gather_done():
        @pl.loop(0, PARTS)
        def _(p):
            all_others(gather_send.at[p])

    sent.append(gather_done)
    row = lax.broadcasted_iota(jnp.int32, (HD, 2 * HD), 0)
    col = lax.broadcasted_iota(jnp.int32, (HD, 2 * HD), 1)
    band = (col > row) & (col <= row + HD)
    causal_even = (col >= HD) & (col <= row + HD)
    causal_odd = col <= row + HD
    lane = col[:, :HD]
    lower = lane <= row[:, :HD]

    acc_a[...] = jnp.zeros_like(acc_a)
    acc_b[...] = jnp.zeros_like(acc_b)
    told[...] = jnp.zeros_like(told)
    kept[...] = jnp.zeros_like(kept)
    own_peak[...] = jnp.zeros_like(own_peak)
    own_sum[...] = jnp.zeros_like(own_sum)

    def scores(q_low_high, keys):
        return dot(q_low_high[:, HD:], keys[:, :HD], 1, 1) + dot(q_low_high, keys, 1, 1)

    def block(h, n):
        here = slice(n * HD, (n + 1) * HD)
        both = slice(max(n - 1, 0) * HD, (n + 1) * HD)
        allowed = band if n else lower
        causal = (causal_odd if n % 2 else causal_even) if n else lower
        s = scores(q2[h, here, :], k2[h, both, :])
        masked = jnp.where(allowed, s, -jnp.inf)
        biggest = jnp.max(masked, axis=1, keepdims=True)
        weights = jnp.exp((masked - biggest) * factor)
        weight_sum = jnp.sum(weights, axis=1, keepdims=True)
        inner = jnp.where(causal, s, 0.0)
        stacked = jnp.concatenate(split(weights) + split(inner), axis=0)
        r = dot(stacked, v2[h, both, :], 1, 0)
        win = r[:HD, :HD] + (r[:HD, HD:] + r[HD : 2 * HD, :HD])
        lin = r[2 * HD : 3 * HD, :HD] + (r[2 * HD : 3 * HD, HD:] + r[3 * HD :, :HD])
        if n:
            a = win * (gain[0, h] / weight_sum)
            a_buf[h, here, :] = a
            acc_a[here, :] += a * a
        else:
            a_buf[h, here, :] = win
            own_peak[...] = jnp.where(lane == h, biggest, own_peak[...])
            own_sum[...] = jnp.where(lane == h, weight_sum, own_sum[...])
        return lin

    def inner_blocks(h):
        load(q_hbm, qbuf, 2, h).wait()
        q_high, q_low = split(qbuf[h])
        q2[h, :, :HD] = q_low
        q2[h, :, HD:] = q_high
        mid = rows // 2
        carried = dot(q2[h, mid:, :], wide(first[h]), 1, 0)
        carried = carried[:, :HD] + carried[:, HD:]
        for n in range(blocks):
            lin = block(h, n)
            if n * HD >= mid:
                lin = lin + carried[n * HD - mid : (n + 1) * HD - mid]
            b_buf[h, n * HD : (n + 1) * HD, :] = lin

    def partial(h, q_high, q_low, keys, vals, target, tile):
        s = scores(jnp.concatenate([q_low, q_high], axis=1), keys)
        biggest = jnp.max(jnp.where(lower, -3e38, s), axis=1, keepdims=True)
        weights = jnp.where(lower, 0.0, jnp.exp((s - biggest) * factor))
        weight_sum = jnp.sum(weights, axis=1, keepdims=True)
        r = dot(jnp.concatenate(split(weights), axis=0), vals, 1, 0)
        target[:, h % 2 * HD : (h % 2 + 1) * HD] = r[:HD, :HD] + (r[:HD, HD:] + r[HD:, :HD])
        tile[...] = jnp.where(lane == h, biggest, jnp.where(lane == heads + h, weight_sum, tile[...]))

    def answer_group(g):
        ask_copy(g).wait_recv()
        for h in (2 * g, 2 * g + 1):
            q_high, q_low = split(asked[g, :, h % 2 * HD : (h % 2 + 1) * HD])
            partial(h, q_high, q_low, k2[h, last, :], v2[h, last, :], answer.at[g], told)
        answer_copy(g).start()

    def keep_group(_):
        for slot in range(2):
            halo_copy(slot).wait_recv()
        for h in (2 * groups, 2 * groups + 1):
            columns = slice(h % 2 * HD, (h % 2 + 1) * HD)
            keys = jnp.concatenate(split(halo[0, :, columns]), axis=1)
            vals = jnp.concatenate(split(halo[1, :, columns]), axis=1)
            q_low_high = q2[h, :HD, :]
            partial(h, q_low_high[:, HD:], q_low_high[:, :HD], keys, vals, answered.at[groups], kept)

    def return_prefixes(j):
        all_others(gather_recv.at[j])
        running = jnp.zeros((depth, HD), F32)
        for c in range(chips):
            prefix[j, c] = running
            if c < chips - 1:
                running = running + gather[j, c]
        piece_in[j, piece(mine), :] = prefix[j, mine]
        for other in others:
            prefix_copy(j, other).start()

    def prefix_done():
        @pl.loop(0, PARTS)
        def _(p):
            all_others(prefix_send.at[p])

    sent.append(prefix_done)

    def cross_copy(j):
        return pltpu.make_async_remote_copy(
            src_ref=cross.at[j],
            dst_ref=state.at[half * core + j],
            send_sem=cross_send.at[j],
            recv_sem=cross_recv.at[j],
            device_id=sibling,
            device_id_type=MESH,
        )

    def forward(j):
        h = half * core + j
        p, e = j // each, j % each
        if e == 0:
            all_others(prefix_recv.at[p])
        before = piece_in[p, e * HD : (e + 1) * HD, :]
        state[h] = before + jnp.where(core == 1, pair[j], 0.0)
        cross[j] = before + jnp.where(core == 0, total[h], 0.0)
        cross_copy(j).start()

    def inner_pair(h):
        @pl.loop(h, h + 2)
        def _(each):
            inner_blocks(each)

    steps = {"v": send_halo, "k": keep_group, "q": ask, "i": inner_blocks, "d": inner_pair, "a": answer_group, "p": return_prefixes, "f": forward}
    for name, which in ORDER:
        steps[name](which)

    def cross_done():
        @pl.loop(0, half)
        def _(j):
            cross_copy(j).wait_send()

    sent.append(cross_done)

    def answer_done():
        @pl.loop(0, groups)
        def _(g):
            answer_copy(g).wait_send()

        told_copy().wait_send()

    told_copy().start()
    sent.append(answer_done)

    def merge():
        for g in range(groups):
            answer_copy(g).wait_recv()
        told_copy().wait_recv()
        peak = own_peak[...]
        other = heard[...] + kept[...]
        other_peak = jnp.where(ctx > 0, other, -3e38)
        other_sum = pltpu.roll(other, HD - heads, 1)
        biggest = jnp.maximum(peak, other_peak)
        scale = jnp.exp((peak - biggest) * factor)
        other_scale = jnp.where(ctx > 0, jnp.exp((other_peak - biggest) * factor), 0.0)
        whole = own_sum[...] * scale + other_sum * other_scale
        scale = scale / whole
        other_scale = other_scale / whole
        square = acc_a[:HD, :]
        for h in range(heads):
            columns = slice(h % 2 * HD, (h % 2 + 1) * HD)
            a = a_buf[h, :HD, :] * scale[:, h : h + 1]
            a = (a + answered[h // 2, :, columns] * other_scale[:, h : h + 1]) * gain[0, h]
            a_buf[h, :HD, :] = a
            square = square + a * a
        acc_a[:HD, :] = square

    def last_linear(h):
        r = dot(q2[h], wide(state[h]), 1, 0)
        b = (b_buf[h] + (r[:, :HD] + r[:, HD:])) * gain[1, h]
        b_buf[h] = b
        acc_b[...] += b * b

    @pl.loop(0, half)
    def _(j):
        last_linear(half * core + j)

    merge()

    def block_sums(acc):
        turned = [jnp.transpose(acc[n * HD : (n + 1) * HD, :]) for n in range(blocks)]
        return [jnp.sum(t, axis=0, keepdims=True) for t in turned]

    sums = block_sums(acc_a)

    @pl.loop(0, half)
    def _(j):
        cross_copy(j).wait_recv()
        last_linear(half * (1 - core) + j)

    sums = sums + block_sums(acc_b)
    sums = jnp.concatenate(sums, axis=0)
    zsend[...] = sums
    zbuf[z] = sums

    def z_copy(d):
        return pltpu.make_async_remote_copy(
            src_ref=zsend,
            dst_ref=zbuf.at[z],
            send_sem=z_send,
            recv_sem=z_recv,
            device_id=(ctx, lax.rem(z + d, head_axis)),
            device_id_type=MESH,
        )

    def z_wait(semaphore):
        sample = zbuf.at[pl.ds(0, head_axis - 1)]
        pltpu.make_async_copy(sample, sample, semaphore).wait()

    for d in sorted(range(1, head_axis), key=lambda d: -min(d, head_axis - d)):
        z_copy(d).start()
    sent.append(lambda: z_wait(z_send))
    z_wait(z_recv)
    squares = zbuf[0]
    for other in range(1, head_axis):
        squares = squares + zbuf[other]
    inverse = 1.0 / jnp.sqrt(squares / (heads * head_axis * HD) + 1e-06)
    inverse = jnp.concatenate([inverse, jnp.zeros((HD - 2 * blocks, HD), F32)], axis=0)
    columns = jnp.transpose(inverse)
    for n in range(blocks):
        here = slice(n * HD, (n + 1) * HD)
        scale_a = columns[:, n : n + 1]
        scale_b = columns[:, blocks + n : blocks + n + 1]
        for h in range(heads):
            out[here, h * HD : (h + 1) * HD] = a_buf[h, here, :] * scale_a + b_buf[h, here, :] * scale_b

    for finish in sent:
        finish()


def shards(ctx_count, head_axis, queries, keys, values, head_gain):
    rows = queries.shape[0]
    heads = head_gain.shape[1]
    chips = ctx_count // 2
    half = heads // 2
    each = half // PARTS
    depth = each * HD // chips
    blocks = rows // HD
    anywhere = pl.BlockSpec(memory_space=pl.ANY)
    dma = pltpu.SemaphoreType.DMA
    vmem = pltpu.VMEM
    body = functools.partial(kernel, ctx_count, head_axis, heads, rows)
    return pl.pallas_call(
        body,
        out_shape=pltpu.VMEM((rows, heads * HD), F32),
        in_specs=[anywhere, anywhere, anywhere, pl.BlockSpec(memory_space=pltpu.SMEM)],
        out_specs=pl.BlockSpec(memory_space=pltpu.VMEM),
        scratch_shapes=[
            vmem((heads, rows, HD), F32),
            vmem((heads, rows, HD), F32),
            vmem((heads, rows, HD), F32),
            vmem((heads // 2 - 1, HD, 2 * HD), F32),
            vmem((heads // 2 - 1, HD, 2 * HD), F32),
            vmem((heads // 2, HD, 2 * HD), F32),
            vmem((2, HD, 2 * HD), F32),
            vmem((HD, HD), F32),
            vmem((HD, HD), F32),
            vmem((HD, HD), F32),
            vmem((HD, HD), F32),
            vmem((HD, HD), F32),
            vmem((heads, rows, 2 * HD), BF16),
            vmem((heads, rows, 2 * HD), BF16),
            vmem((heads, rows, 2 * HD), BF16),
            vmem((heads, HD, HD), F32),
            vmem((heads, HD, HD), F32),
            vmem((half, HD, HD), F32),
            vmem((PARTS, each * HD, HD), F32),
            vmem((PARTS, chips, depth, HD), F32),
            vmem((PARTS, chips, depth, HD), F32),
            vmem((PARTS, each * HD, HD), F32),
            vmem((heads, HD, HD), F32),
            vmem((half, HD, HD), F32),
            vmem((heads, rows, HD), F32),
            vmem((heads, rows, HD), F32),
            vmem((rows, HD), F32),
            vmem((rows, HD), F32),
            vmem((2 * blocks, HD), F32),
            vmem((head_axis, 2 * blocks, HD), F32),
            dma((3, heads)),
            dma((2,)),
            dma((2,)),
            dma((heads // 2,)),
            dma((heads // 2,)),
            dma((heads // 2,)),
            dma((heads // 2,)),
            dma,
            dma,
            dma((half,)),
            dma((half,)),
            dma((PARTS,)),
            dma((PARTS,)),
            dma((PARTS,)),
            dma((PARTS,)),
            dma((half,)),
            dma((half,)),
            dma,
            dma,
        ],
        compiler_params=pltpu.CompilerParams(
            collective_id=0, has_side_effects=True, vmem_limit_bytes=60 * 1024 * 1024
        ),
    )(queries, keys, values, head_gain)


def solution(mesh):
    body = functools.partial(shards, mesh.shape["ctx"], mesh.shape["head"])
    in_specs = (P("ctx", "head"), P("ctx", "head"), P("ctx", "head"), P(None, "head"))
    return jax.shard_map(body, mesh=mesh, in_specs=in_specs, out_specs=P("ctx", "head"), check_vma=False)
```

```python
import functools
import math

import jax
import jax.numpy as jnp
from jax import lax
from jax.experimental import pallas as pl
from jax.experimental.pallas import tpu as pltpu
from jax.sharding import PartitionSpec as P

HEADS = 64
HD = 128
WINDOW = 128
MESH = pl.DeviceIdType.MESH
PARTS = 2
START = (("v", 0), ("q", 0), ("q", 1),)
ORDER = (("q", 2), ("i", 0), ("i", 1), ("i", 2), ("i", 3), ("p", 0), ("a", 0), ("i", 4), ("p", 1), ("a", 1), ("i", 5), ("a", 2), ("i", 6), ("i", 7), ("k", 0), ("f", 0), ("f", 1), ("f", 2), ("f", 3),)
F32 = jnp.float32
BF16 = jnp.bfloat16


def split(x):
    high = x.astype(BF16)
    low = (x - high.astype(F32)).astype(BF16)
    return high, low


def dot(a, b, ca, cb):
    return lax.dot_general(a, b, (((ca,), (cb,)), ((), ())), preferred_element_type=F32)


def wide(x):
    both = jnp.concatenate(split(x), axis=1)
    return jnp.concatenate([both, both], axis=0)


def kernel(
    ctx_count, head_axis, heads, rows,
    q_hbm, k_hbm, v_hbm, gain,
    out,
    kbuf, vbuf, qbuf, asked, answer, answered, halo, told, heard, kept, own_peak, own_sum, k2, v2, q2, first, total, pair, chip, gather, prefix, piece_in, state, cross,
    a_buf, b_buf, acc_a, acc_b, zsend, zbuf,
    load_sem, halo_send, halo_recv, ask_send, ask_recv, answer_send, answer_recv, told_send, told_recv, pair_send, pair_recv, gather_send, gather_recv,
    prefix_send, prefix_recv, cross_send, cross_recv, z_send, z_recv,
):
    ctx = lax.axis_index("ctx")
    z = lax.axis_index("head")
    core = lax.rem(ctx, 2)
    mine = lax.div(ctx, 2)
    chips = ctx_count // 2
    half = heads // 2
    each = half // PARTS
    depth = each * HD // chips
    blocks = rows // HD
    factor = 1.0 / math.sqrt(HD)
    sibling = (ctx + 1 - 2 * core, z)
    following = (lax.rem(ctx + 1, ctx_count), z)
    preceding = (lax.rem(ctx + ctx_count - 1, ctx_count), z)
    side = math.isqrt(chips)
    my_y, my_x = lax.div(mine, side), lax.rem(mine, side)
    others = []
    for dy in range(side):
        for dx in range(side):
            hops = min(dx, side - dx) + min(dy, side - dy)
            if hops:
                other = lax.rem(my_y + dy, side) * side + lax.rem(my_x + dx, side)
                others.append((hops, len(others), other))
    others = [other for _, _, other in sorted(others, key=lambda o: (-o[0], o[1]))]

    def piece(c):
        return pl.ds(pl.multiple_of(c * depth, depth), depth)

    def load(source, target, slot, h):
        columns = pl.ds(pl.multiple_of(h * HD, HD), HD)
        return pltpu.make_async_copy(source.at[:, columns], target.at[h], load_sem.at[slot, h])

    sent = []
    has_before = ctx > 0
    has_after = ctx < ctx_count - 1

    def when(condition, *actions):
        @pl.when(condition)
        def _():
            for action in actions:
                action()


    barrier = pltpu.get_barrier_semaphore()

    def greet(device):
        pl.semaphore_signal(barrier, inc=1, device_id=device, device_id_type=MESH)

    for jj in range(heads):
        h = lax.rem(jj + half * (1 - core), heads)
        load(k_hbm, kbuf, 0, h).start()
        load(v_hbm, vbuf, 1, h).start()
    greet(following)
    greet(preceding)
    greet(sibling)
    for other in others:
        greet((2 * other + core, z))
    for d in range(1, head_axis):
        greet((ctx, lax.rem(z + d, head_axis)))
    for h in range(heads):
        load(q_hbm, qbuf, 2, h).start()
    groups = heads // 2 - 1
    last = slice(rows - HD, rows)

    def ask_copy(g):
        return pltpu.make_async_remote_copy(
            src_ref=q_hbm.at[pl.ds(0, HD), pl.ds(pl.multiple_of(g * 2 * HD, HD), 2 * HD)],
            dst_ref=asked.at[g],
            send_sem=ask_send.at[g],
            recv_sem=ask_recv.at[g],
            device_id=preceding,
            device_id_type=MESH,
        )

    def answer_copy(g):
        return pltpu.make_async_remote_copy(
            src_ref=answer.at[g],
            dst_ref=answered.at[g],
            send_sem=answer_send.at[g],
            recv_sem=answer_recv.at[g],
            device_id=following,
            device_id_type=MESH,
        )

    kept_columns = pl.ds(groups * 2 * HD, 2 * HD)

    def halo_copy(slot):
        return pltpu.make_async_remote_copy(
            src_ref=(k_hbm, v_hbm)[slot].at[pl.ds(rows - HD, HD), kept_columns],
            dst_ref=halo.at[slot],
            send_sem=halo_send.at[slot],
            recv_sem=halo_recv.at[slot],
            device_id=following,
            device_id_type=MESH,
        )

    def send_halo(_):
        when(has_after, *[halo_copy(slot).start for slot in range(2)])

    def ask(g):
        when(has_before, ask_copy(g).start)

    def told_copy():
        return pltpu.make_async_remote_copy(
            src_ref=told,
            dst_ref=heard,
            send_sem=told_send,
            recv_sem=told_recv,
            device_id=following,
            device_id_type=MESH,
        )

    def local_state(h):
        load(k_hbm, kbuf, 0, h).wait()
        load(v_hbm, vbuf, 1, h).wait()
        k_high, k_low = split(kbuf[h])
        v_high, v_low = split(vbuf[h])
        k2[h, :, :HD] = k_high
        k2[h, :, HD:] = k_low
        v2[h, :, :HD] = v_high
        v2[h, :, HD:] = v_low
        kk = jnp.concatenate([k_high, k_low], axis=1)
        vv = jnp.concatenate([v_high, v_low], axis=1)
        mid = rows // 2
        parts = []
        for part in range(2):
            r = dot(kk[part * mid : (part + 1) * mid], vv[part * mid : (part + 1) * mid], 0, 0)
            parts.append(r[:HD, :HD] + (r[:HD, HD:] + r[HD:, :HD]))
        first[h] = parts[0]
        total[h] = parts[0] + parts[1]

    def pair_copy(j):
        return pltpu.make_async_remote_copy(
            src_ref=total.at[half * (1 - core) + j],
            dst_ref=pair.at[j],
            send_sem=pair_send.at[j],
            recv_sem=pair_recv.at[j],
            device_id=sibling,
            device_id_type=MESH,
        )

    def gather_copy(j, target):
        return pltpu.make_async_remote_copy(
            src_ref=chip.at[j, piece(target), :],
            dst_ref=gather.at[j, mine],
            send_sem=gather_send.at[j],
            recv_sem=gather_recv.at[j],
            device_id=(2 * target + core, z),
            device_id_type=MESH,
        )

    def prefix_copy(j, target):
        return pltpu.make_async_remote_copy(
            src_ref=prefix.at[j, target],
            dst_ref=piece_in.at[j, piece(mine), :],
            send_sem=prefix_send.at[j],
            recv_sem=prefix_recv.at[j],
            device_id=(2 * target + core, z),
            device_id_type=MESH,
        )

    def all_others(semaphore):
        sample = gather.at[0, pl.ds(0, chips - 1)]
        pltpu.make_async_copy(sample, sample, semaphore).wait()

    @pl.loop(0, half)
    def _(j):
        local_state(half * (1 - core) + j)

    pl.semaphore_wait(barrier, 3 + chips - 1 + head_axis - 1)
    for j in range(half):
        pair_copy(j).start()
    for name, which in START:
        {"v": send_halo, "q": ask}[name](which)
    sent.append(lambda: when(has_before, *[ask_copy(g).wait_send for g in range(groups)]))
    sent.append(lambda: when(has_after, *[halo_copy(slot).wait_send for slot in range(2)]))

    def pair_done():
        @pl.loop(0, half)
        def _(j):
            pair_copy(j).wait_send()

    sent.append(pair_done)

    @pl.loop(0, PARTS)
    def _(p):
        for e in range(each):
            j = p * each + e
            h = half * core + j
            local_state(h)
            pair_copy(j).wait_recv()
            chip[p, e * HD : (e + 1) * HD, :] = total[h] + pair[j]
        gather[p, mine] = chip[p, piece(mine), :]
        for other in others:
            gather_copy(p, other).start()

    def gather_done():
        @pl.loop(0, PARTS)
        def _(p):
            all_others(gather_send.at[p])

    sent.append(gather_done)
    row = lax.broadcasted_iota(jnp.int32, (HD, 2 * HD), 0)
    col = lax.broadcasted_iota(jnp.int32, (HD, 2 * HD), 1)
    band = (col > row) & (col <= row + HD)
    causal_even = (col >= HD) & (col <= row + HD)
    causal_odd = col <= row + HD
    lane = col[:, :HD]
    lower = lane <= row[:, :HD]

    acc_a[...] = jnp.zeros_like(acc_a)
    acc_b[...] = jnp.zeros_like(acc_b)
    told[...] = jnp.zeros_like(told)
    kept[...] = jnp.zeros_like(kept)
    own_peak[...] = jnp.zeros_like(own_peak)

    @pl.when(ctx == 0)
    def _():
        answered[...] = jnp.zeros_like(answered)
        heard[...] = jnp.zeros_like(heard)
        halo[...] = jnp.zeros_like(halo)

    @pl.when(ctx == ctx_count - 1)
    def _():
        asked[...] = jnp.zeros_like(asked)

    own_sum[...] = jnp.zeros_like(own_sum)

    def scores(q_low_high, keys):
        return dot(q_low_high[:, HD:], keys[:, :HD], 1, 1) + dot(q_low_high, keys, 1, 1)

    def block(h, n):
        here = slice(n * HD, (n + 1) * HD)
        both = slice(max(n - 1, 0) * HD, (n + 1) * HD)
        allowed = band if n else lower
        causal = (causal_odd if n % 2 else causal_even) if n else lower
        s = scores(q2[h, here, :], k2[h, both, :])
        masked = jnp.where(allowed, s, -jnp.inf)
        biggest = jnp.max(masked, axis=1, keepdims=True)
        weights = jnp.exp((masked - biggest) * factor)
        weight_sum = jnp.sum(weights, axis=1, keepdims=True)
        inner = jnp.where(causal, s, 0.0)
        stacked = jnp.concatenate(split(weights) + split(inner), axis=0)
        r = dot(stacked, v2[h, both, :], 1, 0)
        win = r[:HD, :HD] + (r[:HD, HD:] + r[HD : 2 * HD, :HD])
        lin = r[2 * HD : 3 * HD, :HD] + (r[2 * HD : 3 * HD, HD:] + r[3 * HD :, :HD])
        if n:
            a = win * (gain[0, h] / weight_sum)
            a_buf[h, here, :] = a
            acc_a[here, :] += a * a
        else:
            a_buf[h, here, :] = win
            own_peak[...] = jnp.where(lane == h, biggest, own_peak[...])
            own_sum[...] = jnp.where(lane == h, weight_sum, own_sum[...])
        return lin

    def inner_blocks(h):
        load(q_hbm, qbuf, 2, h).wait()
        q_high, q_low = split(qbuf[h])
        q2[h, :, :HD] = q_low
        q2[h, :, HD:] = q_high
        mid = rows // 2
        carried = dot(q2[h, mid:, :], wide(first[h]), 1, 0)
        carried = carried[:, :HD] + carried[:, HD:]
        for n in range(blocks):
            lin = block(h, n)
            if n * HD >= mid:
                lin = lin + carried[n * HD - mid : (n + 1) * HD - mid]
            b_buf[h, n * HD : (n + 1) * HD, :] = lin

    def partial(h, q_high, q_low, keys, vals, target, tile):
        s = scores(jnp.concatenate([q_low, q_high], axis=1), keys)
        biggest = jnp.max(jnp.where(lower, -3e38, s), axis=1, keepdims=True)
        weights = jnp.where(lower, 0.0, jnp.exp((s - biggest) * factor))
        weight_sum = jnp.sum(weights, axis=1, keepdims=True)
        r = dot(jnp.concatenate(split(weights), axis=0), vals, 1, 0)
        target[:, h % 2 * HD : (h % 2 + 1) * HD] = r[:HD, :HD] + (r[:HD, HD:] + r[HD:, :HD])
        tile[...] = jnp.where(lane == h, biggest, jnp.where(lane == heads + h, weight_sum, tile[...]))

    def answer_group(g):
        when(has_after, ask_copy(g).wait_recv)
        for h in (2 * g, 2 * g + 1):
            q_high, q_low = split(asked[g, :, h % 2 * HD : (h % 2 + 1) * HD])
            partial(h, q_high, q_low, k2[h, last, :], v2[h, last, :], answer.at[g], told)
        when(has_after, answer_copy(g).start)

    def keep_group(_):
        when(has_before, *[halo_copy(slot).wait_recv for slot in range(2)])
        for h in (2 * groups, 2 * groups + 1):
            columns = slice(h % 2 * HD, (h % 2 + 1) * HD)
            keys = jnp.concatenate(split(halo[0, :, columns]), axis=1)
            vals = jnp.concatenate(split(halo[1, :, columns]), axis=1)
            q_low_high = q2[h, :HD, :]
            partial(h, q_low_high[:, HD:], q_low_high[:, :HD], keys, vals, answered.at[groups], kept)

    def return_prefixes(j):
        all_others(gather_recv.at[j])
        running = jnp.zeros((depth, HD), F32)
        for c in range(chips):
            prefix[j, c] = running
            if c < chips - 1:
                running = running + gather[j, c]
        piece_in[j, piece(mine), :] = prefix[j, mine]
        for other in others:
            prefix_copy(j, other).start()

    def prefix_done():
        @pl.loop(0, PARTS)
        def _(p):
            all_others(prefix_send.at[p])

    sent.append(prefix_done)

    def cross_copy(j):
        return pltpu.make_async_remote_copy(
            src_ref=cross.at[j],
            dst_ref=state.at[half * core + j],
            send_sem=cross_send.at[j],
            recv_sem=cross_recv.at[j],
            device_id=sibling,
            device_id_type=MESH,
        )

    def forward(j):
        h = half * core + j
        p, e = j // each, j % each
        if e == 0:
            all_others(prefix_recv.at[p])
        before = piece_in[p, e * HD : (e + 1) * HD, :]
        state[h] = before + jnp.where(core == 1, pair[j], 0.0)
        cross[j] = before + jnp.where(core == 0, total[h], 0.0)
        cross_copy(j).start()

    def inner_pair(h):
        @pl.loop(h, h + 2)
        def _(each):
            inner_blocks(each)

    steps = {"v": send_halo, "k": keep_group, "q": ask, "i": inner_blocks, "d": inner_pair, "a": answer_group, "p": return_prefixes, "f": forward}
    for name, which in ORDER:
        steps[name](which)

    def cross_done():
        @pl.loop(0, half)
        def _(j):
            cross_copy(j).wait_send()

    sent.append(cross_done)

    def answer_done():
        when(has_after, told_copy().wait_send, *[answer_copy(g).wait_send for g in range(groups)])

    when(has_after, told_copy().start)
    sent.append(answer_done)

    def merge():
        when(has_before, told_copy().wait_recv, *[answer_copy(g).wait_recv for g in range(groups)])
        peak = own_peak[...]
        other = heard[...] + kept[...]
        other_peak = jnp.where(ctx > 0, other, -3e38)
        other_sum = pltpu.roll(other, HD - heads, 1)
        biggest = jnp.maximum(peak, other_peak)
        scale = jnp.exp((peak - biggest) * factor)
        other_scale = jnp.where(ctx > 0, jnp.exp((other_peak - biggest) * factor), 0.0)
        whole = own_sum[...] * scale + other_sum * other_scale
        scale = scale / whole
        other_scale = other_scale / whole
        square = acc_a[:HD, :]
        for h in range(heads):
            columns = slice(h % 2 * HD, (h % 2 + 1) * HD)
            a = a_buf[h, :HD, :] * scale[:, h : h + 1]
            a = (a + answered[h // 2, :, columns] * other_scale[:, h : h + 1]) * gain[0, h]
            a_buf[h, :HD, :] = a
            square = square + a * a
        acc_a[:HD, :] = square

    def last_linear(h):
        r = dot(q2[h], wide(state[h]), 1, 0)
        b = (b_buf[h] + (r[:, :HD] + r[:, HD:])) * gain[1, h]
        b_buf[h] = b
        acc_b[...] += b * b

    @pl.loop(0, half)
    def _(j):
        last_linear(half * core + j)

    merge()

    def block_sums(acc):
        turned = [jnp.transpose(acc[n * HD : (n + 1) * HD, :]) for n in range(blocks)]
        return [jnp.sum(t, axis=0, keepdims=True) for t in turned]

    sums = block_sums(acc_a)

    @pl.loop(0, half)
    def _(j):
        cross_copy(j).wait_recv()
        last_linear(half * (1 - core) + j)

    sums = sums + block_sums(acc_b)
    sums = jnp.concatenate(sums, axis=0)
    zsend[...] = sums
    zbuf[z] = sums

    def z_copy(d):
        return pltpu.make_async_remote_copy(
            src_ref=zsend,
            dst_ref=zbuf.at[z],
            send_sem=z_send,
            recv_sem=z_recv,
            device_id=(ctx, lax.rem(z + d, head_axis)),
            device_id_type=MESH,
        )

    def z_wait(semaphore):
        sample = zbuf.at[pl.ds(0, head_axis - 1)]
        pltpu.make_async_copy(sample, sample, semaphore).wait()

    for d in sorted(range(1, head_axis), key=lambda d: -min(d, head_axis - d)):
        z_copy(d).start()
    sent.append(lambda: z_wait(z_send))
    z_wait(z_recv)
    squares = zbuf[0]
    for other in range(1, head_axis):
        squares = squares + zbuf[other]
    inverse = 1.0 / jnp.sqrt(squares / (heads * head_axis * HD) + 1e-06)
    inverse = jnp.concatenate([inverse, jnp.zeros((HD - 2 * blocks, HD), F32)], axis=0)
    columns = jnp.transpose(inverse)
    for n in range(blocks):
        here = slice(n * HD, (n + 1) * HD)
        scale_a = columns[:, n : n + 1]
        scale_b = columns[:, blocks + n : blocks + n + 1]
        for h in range(heads):
            out[here, h * HD : (h + 1) * HD] = a_buf[h, here, :] * scale_a + b_buf[h, here, :] * scale_b

    for finish in sent:
        finish()


def shards(ctx_count, head_axis, queries, keys, values, head_gain):
    rows = queries.shape[0]
    heads = head_gain.shape[1]
    chips = ctx_count // 2
    half = heads // 2
    each = half // PARTS
    depth = each * HD // chips
    blocks = rows // HD
    anywhere = pl.BlockSpec(memory_space=pl.ANY)
    dma = pltpu.SemaphoreType.DMA
    vmem = pltpu.VMEM
    body = functools.partial(kernel, ctx_count, head_axis, heads, rows)
    return pl.pallas_call(
        body,
        out_shape=pltpu.VMEM((rows, heads * HD), F32),
        in_specs=[anywhere, anywhere, anywhere, pl.BlockSpec(memory_space=pltpu.SMEM)],
        out_specs=pl.BlockSpec(memory_space=pltpu.VMEM),
        scratch_shapes=[
            vmem((heads, rows, HD), F32),
            vmem((heads, rows, HD), F32),
            vmem((heads, rows, HD), F32),
            vmem((heads // 2 - 1, HD, 2 * HD), F32),
            vmem((heads // 2 - 1, HD, 2 * HD), F32),
            vmem((heads // 2, HD, 2 * HD), F32),
            vmem((2, HD, 2 * HD), F32),
            vmem((HD, HD), F32),
            vmem((HD, HD), F32),
            vmem((HD, HD), F32),
            vmem((HD, HD), F32),
            vmem((HD, HD), F32),
            vmem((heads, rows, 2 * HD), BF16),
            vmem((heads, rows, 2 * HD), BF16),
            vmem((heads, rows, 2 * HD), BF16),
            vmem((heads, HD, HD), F32),
            vmem((heads, HD, HD), F32),
            vmem((half, HD, HD), F32),
            vmem((PARTS, each * HD, HD), F32),
            vmem((PARTS, chips, depth, HD), F32),
            vmem((PARTS, chips, depth, HD), F32),
            vmem((PARTS, each * HD, HD), F32),
            vmem((heads, HD, HD), F32),
            vmem((half, HD, HD), F32),
            vmem((heads, rows, HD), F32),
            vmem((heads, rows, HD), F32),
            vmem((rows, HD), F32),
            vmem((rows, HD), F32),
            vmem((2 * blocks, HD), F32),
            vmem((head_axis, 2 * blocks, HD), F32),
            dma((3, heads)),
            dma((2,)),
            dma((2,)),
            dma((heads // 2,)),
            dma((heads // 2,)),
            dma((heads // 2,)),
            dma((heads // 2,)),
            dma,
            dma,
            dma((half,)),
            dma((half,)),
            dma((PARTS,)),
            dma((PARTS,)),
            dma((PARTS,)),
            dma((PARTS,)),
            dma((half,)),
            dma((half,)),
            dma,
            dma,
        ],
        compiler_params=pltpu.CompilerParams(
            collective_id=0, has_side_effects=True, vmem_limit_bytes=60 * 1024 * 1024
        ),
    )(queries, keys, values, head_gain)


def solution(mesh):
    body = functools.partial(shards, mesh.shape["ctx"], mesh.shape["head"])
    in_specs = (P("ctx", "head"), P("ctx", "head"), P("ctx", "head"), P(None, "head"))
    return jax.shard_map(body, mesh=mesh, in_specs=in_specs, out_specs=P("ctx", "head"), check_vma=False)
```

```python
import functools
import math

import jax
import jax.numpy as jnp
from jax import lax
from jax.experimental import pallas as pl
from jax.experimental.pallas import tpu as pltpu
from jax.sharding import PartitionSpec as P

HEADS = 64
HD = 128
WINDOW = 128
MESH = pl.DeviceIdType.MESH
PARTS = 2
START = (("v", 0), ("q", 0), ("q", 1),)
ORDER = (("q", 2), ("i", 0), ("i", 1), ("i", 2), ("i", 3), ("p", 0), ("a", 0), ("i", 4), ("p", 1), ("a", 1), ("i", 5), ("a", 2), ("i", 6), ("i", 7), ("k", 0), ("f", 0), ("f", 1), ("f", 2), ("f", 3),)
F32 = jnp.float32
BF16 = jnp.bfloat16


def split(x):
    high = x.astype(BF16)
    low = (x - high.astype(F32)).astype(BF16)
    return high, low


def dot(a, b, ca, cb):
    return lax.dot_general(a, b, (((ca,), (cb,)), ((), ())), preferred_element_type=F32)


def wide(x):
    both = jnp.concatenate(split(x), axis=1)
    return jnp.concatenate([both, both], axis=0)


def kernel(
    ctx_count, head_axis, heads, rows,
    q_hbm, k_hbm, v_hbm, gain,
    out,
    kbuf, vbuf, qbuf, asked, answer, answered, halo, told, heard, kept, own_peak, own_sum, k2, v2, q2, first, total, pair, chip, gather, prefix, piece_in, state, cross,
    a_buf, b_buf, acc_a, acc_b, zsend, zbuf,
    load_sem, halo_send, halo_recv, ask_send, ask_recv, answer_send, answer_recv, told_send, told_recv, pair_send, pair_recv, gather_send, gather_recv,
    prefix_send, prefix_recv, cross_send, cross_recv, z_send, z_recv,
):
    ctx = lax.axis_index("ctx")
    z = lax.axis_index("head")
    core = lax.rem(ctx, 2)
    mine = lax.div(ctx, 2)
    chips = ctx_count // 2
    half = heads // 2
    each = half // PARTS
    depth = each * HD // chips
    blocks = rows // HD
    factor = 1.0 / math.sqrt(HD)
    sibling = (ctx + 1 - 2 * core, z)
    following = (lax.rem(ctx + 1, ctx_count), z)
    preceding = (lax.rem(ctx + ctx_count - 1, ctx_count), z)
    side = math.isqrt(chips)
    my_y, my_x = lax.div(mine, side), lax.rem(mine, side)
    others = []
    for dy in range(side):
        for dx in range(side):
            hops = min(dx, side - dx) + min(dy, side - dy)
            if hops:
                other = lax.rem(my_y + dy, side) * side + lax.rem(my_x + dx, side)
                others.append((hops, len(others), other))
    others = [other for _, _, other in sorted(others, key=lambda o: (-o[0], o[1]))]

    def piece(c):
        return pl.ds(pl.multiple_of(c * depth, depth), depth)

    def load(source, target, slot, h):
        columns = pl.ds(pl.multiple_of(h * HD, HD), HD)
        return pltpu.make_async_copy(source.at[:, columns], target.at[h], load_sem.at[slot, h])

    sent = []
    has_before = ctx > 0
    has_after = ctx < ctx_count - 1

    def when(condition, *actions):
        @pl.when(condition)
        def _():
            for action in actions:
                action()


    barrier = pltpu.get_barrier_semaphore()

    def greet(device):
        pl.semaphore_signal(barrier, inc=1, device_id=device, device_id_type=MESH)

    for jj in range(heads):
        h = lax.rem(jj + half * (1 - core), heads)
        load(k_hbm, kbuf, 0, h).start()
        load(v_hbm, vbuf, 1, h).start()
    greet(following)
    greet(preceding)
    greet(sibling)
    for other in others:
        greet((2 * other + core, z))
    for d in range(1, head_axis):
        greet((ctx, lax.rem(z + d, head_axis)))
    for h in range(heads):
        load(q_hbm, qbuf, 2, h).start()
    groups = heads // 2 - 1
    last = slice(rows - HD, rows)

    def ask_copy(g):
        return pltpu.make_async_remote_copy(
            src_ref=q_hbm.at[pl.ds(0, HD), pl.ds(pl.multiple_of(g * 2 * HD, HD), 2 * HD)],
            dst_ref=asked.at[g],
            send_sem=ask_send.at[g],
            recv_sem=ask_recv.at[g],
            device_id=preceding,
            device_id_type=MESH,
        )

    def answer_copy(g):
        return pltpu.make_async_remote_copy(
            src_ref=answer.at[g],
            dst_ref=answered.at[g],
            send_sem=answer_send.at[g],
            recv_sem=answer_recv.at[g],
            device_id=following,
            device_id_type=MESH,
        )

    kept_columns = pl.ds(groups * 2 * HD, 2 * HD)

    def halo_copy(slot):
        return pltpu.make_async_remote_copy(
            src_ref=(k_hbm, v_hbm)[slot].at[pl.ds(rows - HD, HD), kept_columns],
            dst_ref=halo.at[slot],
            send_sem=halo_send.at[slot],
            recv_sem=halo_recv.at[slot],
            device_id=following,
            device_id_type=MESH,
        )

    def send_halo(_):
        when(has_after, *[halo_copy(slot).start for slot in range(2)])

    def ask(g):
        when(has_before, ask_copy(g).start)

    def told_copy():
        return pltpu.make_async_remote_copy(
            src_ref=told,
            dst_ref=heard,
            send_sem=told_send,
            recv_sem=told_recv,
            device_id=following,
            device_id_type=MESH,
        )

    def local_state(h):
        load(k_hbm, kbuf, 0, h).wait()
        load(v_hbm, vbuf, 1, h).wait()
        k_high, k_low = split(kbuf[h])
        v_high, v_low = split(vbuf[h])
        k2[h, :, :HD] = k_high
        k2[h, :, HD:] = k_low
        v2[h, :, :HD] = v_high
        v2[h, :, HD:] = v_low
        kk = jnp.concatenate([k_high, k_low], axis=1)
        vv = jnp.concatenate([v_high, v_low], axis=1)
        mid = rows // 2
        parts = []
        for part in range(2):
            r = dot(kk[part * mid : (part + 1) * mid], vv[part * mid : (part + 1) * mid], 0, 0)
            parts.append(r[:HD, :HD] + (r[:HD, HD:] + r[HD:, :HD]))
        first[h] = parts[0]
        total[h] = parts[0] + parts[1]

    def pair_copy(j):
        return pltpu.make_async_remote_copy(
            src_ref=total.at[half * (1 - core) + j],
            dst_ref=pair.at[j],
            send_sem=pair_send.at[j],
            recv_sem=pair_recv.at[j],
            device_id=sibling,
            device_id_type=MESH,
        )

    def gather_copy(j, target):
        return pltpu.make_async_remote_copy(
            src_ref=chip.at[j, piece(target), :],
            dst_ref=gather.at[j, mine],
            send_sem=gather_send.at[j],
            recv_sem=gather_recv.at[j],
            device_id=(2 * target + core, z),
            device_id_type=MESH,
        )

    def prefix_copy(j, target):
        return pltpu.make_async_remote_copy(
            src_ref=prefix.at[j, target],
            dst_ref=piece_in.at[j, piece(mine), :],
            send_sem=prefix_send.at[j],
            recv_sem=prefix_recv.at[j],
            device_id=(2 * target + core, z),
            device_id_type=MESH,
        )

    def all_others(semaphore):
        sample = gather.at[0, pl.ds(0, chips - 1)]
        pltpu.make_async_copy(sample, sample, semaphore).wait()

    @pl.loop(0, half)
    def _(j):
        local_state(half * (1 - core) + j)

    pl.semaphore_wait(barrier, 3 + chips - 1 + head_axis - 1)
    for j in range(half):
        pair_copy(j).start()
    for name, which in START:
        {"v": send_halo, "q": ask}[name](which)
    sent.append(lambda: when(has_before, *[ask_copy(g).wait_send for g in range(groups)]))
    sent.append(lambda: when(has_after, *[halo_copy(slot).wait_send for slot in range(2)]))

    def pair_done():
        @pl.loop(0, half)
        def _(j):
            pair_copy(j).wait_send()

    sent.append(pair_done)

    @pl.loop(0, PARTS)
    def _(p):
        for e in range(each):
            j = p * each + e
            h = half * core + j
            local_state(h)
            pair_copy(j).wait_recv()
            chip[p, e * HD : (e + 1) * HD, :] = total[h] + pair[j]
        gather[p, mine] = chip[p, piece(mine), :]
        for other in others:
            gather_copy(p, other).start()

    def gather_done():
        @pl.loop(0, PARTS)
        def _(p):
            all_others(gather_send.at[p])

    sent.append(gather_done)
    row = lax.broadcasted_iota(jnp.int32, (HD, 2 * HD), 0)
    col = lax.broadcasted_iota(jnp.int32, (HD, 2 * HD), 1)
    band = (col > row) & (col <= row + HD)
    causal_even = (col >= HD) & (col <= row + HD)
    causal_odd = col <= row + HD
    lane = col[:, :HD]
    lower = lane <= row[:, :HD]

    acc_a[...] = jnp.zeros_like(acc_a)
    acc_b[...] = jnp.zeros_like(acc_b)
    told[...] = jnp.zeros_like(told)
    kept[...] = jnp.zeros_like(kept)
    own_peak[...] = jnp.zeros_like(own_peak)

    @pl.when(ctx == 0)
    def _():
        answered[...] = jnp.zeros_like(answered)
        heard[...] = jnp.zeros_like(heard)
        halo[...] = jnp.zeros_like(halo)

    @pl.when(ctx == ctx_count - 1)
    def _():
        asked[...] = jnp.zeros_like(asked)

    own_sum[...] = jnp.zeros_like(own_sum)

    def scores(q_low_high, keys):
        return dot(q_low_high[:, HD:], keys[:, :HD], 1, 1) + dot(q_low_high, keys, 1, 1)

    def block(h, n):
        here = slice(n * HD, (n + 1) * HD)
        both = slice(max(n - 1, 0) * HD, (n + 1) * HD)
        allowed = band if n else lower
        causal = (causal_odd if n % 2 else causal_even) if n else lower
        s = scores(q2[h, here, :], k2[h, both, :])
        masked = jnp.where(allowed, s, -jnp.inf)
        biggest = jnp.max(masked, axis=1, keepdims=True)
        weights = jnp.exp((masked - biggest) * factor)
        weight_sum = jnp.sum(weights, axis=1, keepdims=True)
        inner = jnp.where(causal, s, 0.0)
        stacked = jnp.concatenate(split(weights) + split(inner), axis=0)
        r = dot(stacked, v2[h, both, :], 1, 0)
        win = r[:HD, :HD] + (r[:HD, HD:] + r[HD : 2 * HD, :HD])
        lin = r[2 * HD : 3 * HD, :HD] + (r[2 * HD : 3 * HD, HD:] + r[3 * HD :, :HD])
        if n:
            a = win * (gain[0, h] / weight_sum)
            a_buf[h, here, :] = a
            acc_a[here, :] += a * a
        else:
            a_buf[h, here, :] = win
            own_peak[...] = jnp.where(lane == h, biggest, own_peak[...])
            own_sum[...] = jnp.where(lane == h, weight_sum, own_sum[...])
        return lin

    def inner_blocks(h):
        load(q_hbm, qbuf, 2, h).wait()
        q_high, q_low = split(qbuf[h])
        q2[h, :, :HD] = q_low
        q2[h, :, HD:] = q_high
        mid = rows // 2
        carried = dot(q2[h, mid:, :], wide(first[h]), 1, 0)
        carried = carried[:, :HD] + carried[:, HD:]
        for n in range(blocks):
            lin = block(h, n)
            if n * HD >= mid:
                lin = lin + carried[n * HD - mid : (n + 1) * HD - mid]
            b_buf[h, n * HD : (n + 1) * HD, :] = lin

    def partial(h, q_high, q_low, keys, vals, target, tile):
        s = scores(jnp.concatenate([q_low, q_high], axis=1), keys)
        biggest = jnp.max(jnp.where(lower, -3e38, s), axis=1, keepdims=True)
        weights = jnp.where(lower, 0.0, jnp.exp((s - biggest) * factor))
        weight_sum = jnp.sum(weights, axis=1, keepdims=True)
        r = dot(jnp.concatenate(split(weights), axis=0), vals, 1, 0)
        target[:, h % 2 * HD : (h % 2 + 1) * HD] = r[:HD, :HD] + (r[:HD, HD:] + r[HD:, :HD])
        tile[...] = jnp.where(lane == h, biggest, jnp.where(lane == heads + h, weight_sum, tile[...]))

    def answer_group(g):
        when(has_after, ask_copy(g).wait_recv)
        for h in (2 * g, 2 * g + 1):
            q_high, q_low = split(asked[g, :, h % 2 * HD : (h % 2 + 1) * HD])
            partial(h, q_high, q_low, k2[h, last, :], v2[h, last, :], answer.at[g], told)
        when(has_after, answer_copy(g).start)

    def keep_group(_):
        when(has_before, *[halo_copy(slot).wait_recv for slot in range(2)])
        for h in (2 * groups, 2 * groups + 1):
            columns = slice(h % 2 * HD, (h % 2 + 1) * HD)
            keys = jnp.concatenate(split(halo[0, :, columns]), axis=1)
            vals = jnp.concatenate(split(halo[1, :, columns]), axis=1)
            q_low_high = q2[h, :HD, :]
            partial(h, q_low_high[:, HD:], q_low_high[:, :HD], keys, vals, answered.at[groups], kept)

    def return_prefixes(j):
        all_others(gather_recv.at[j])
        running = jnp.zeros((depth, HD), F32)
        for c in range(chips):
            prefix[j, c] = running
            if c < chips - 1:
                running = running + gather[j, c]
        piece_in[j, piece(mine), :] = prefix[j, mine]
        for other in others:
            prefix_copy(j, other).start()

    def prefix_done():
        @pl.loop(0, PARTS)
        def _(p):
            all_others(prefix_send.at[p])

    sent.append(prefix_done)

    def cross_copy(j):
        return pltpu.make_async_remote_copy(
            src_ref=cross.at[j],
            dst_ref=state.at[half * core + j],
            send_sem=cross_send.at[j],
            recv_sem=cross_recv.at[j],
            device_id=sibling,
            device_id_type=MESH,
        )

    def forward(j):
        h = half * core + j
        p, e = j // each, j % each
        if e == 0:
            all_others(prefix_recv.at[p])
        before = piece_in[p, e * HD : (e + 1) * HD, :]
        state[h] = before + jnp.where(core == 1, pair[j], 0.0)
        cross[j] = before + jnp.where(core == 0, total[h], 0.0)
        cross_copy(j).start()

    def inner_pair(h):
        @pl.loop(h, h + 2)
        def _(each):
            inner_blocks(each)

    steps = {"v": send_halo, "k": keep_group, "q": ask, "i": inner_blocks, "d": inner_pair, "a": answer_group, "p": return_prefixes, "f": forward}
    for name, which in ORDER:
        steps[name](which)

    def cross_done():
        @pl.loop(0, half)
        def _(j):
            cross_copy(j).wait_send()

    sent.append(cross_done)

    def answer_done():
        when(has_after, told_copy().wait_send, *[answer_copy(g).wait_send for g in range(groups)])

    when(has_after, told_copy().start)
    sent.append(answer_done)

    def merge():
        when(has_before, told_copy().wait_recv, *[answer_copy(g).wait_recv for g in range(groups)])
        peak = own_peak[...]
        other = heard[...] + kept[...]
        other_peak = jnp.where(ctx > 0, other, -3e38)
        other_sum = pltpu.roll(other, HD - heads, 1)
        biggest = jnp.maximum(peak, other_peak)
        scale = jnp.exp((peak - biggest) * factor)
        other_scale = jnp.where(ctx > 0, jnp.exp((other_peak - biggest) * factor), 0.0)
        whole = own_sum[...] * scale + other_sum * other_scale
        scale = scale / whole
        other_scale = other_scale / whole
        square = acc_a[:HD, :]
        for h in range(heads):
            columns = slice(h % 2 * HD, (h % 2 + 1) * HD)
            a = a_buf[h, :HD, :] * scale[:, h : h + 1]
            a = (a + answered[h // 2, :, columns] * other_scale[:, h : h + 1]) * gain[0, h]
            a_buf[h, :HD, :] = a
            square = square + a * a
        acc_a[:HD, :] = square

    def last_linear(h):
        r = dot(q2[h], wide(state[h]), 1, 0)
        b = (b_buf[h] + (r[:, :HD] + r[:, HD:])) * gain[1, h]
        b_buf[h] = b
        acc_b[...] += b * b

    @pl.loop(0, half)
    def _(j):
        last_linear(half * core + j)

    @pl.loop(0, half)
    def _(j):
        cross_copy(j).wait_recv()
        last_linear(half * (1 - core) + j)

    def block_sum(acc, n):
        return jnp.sum(jnp.transpose(acc[n * HD : (n + 1) * HD, :]), axis=0, keepdims=True)

    sums = [block_sum(acc_a, n) for n in range(1, blocks)] + [block_sum(acc_b, n) for n in range(blocks)]
    zsend[1:, :] = jnp.concatenate(sums, axis=0)
    merge()
    zsend[:1, :] = block_sum(acc_a, 0)
    sums = zsend[...]
    zbuf[z] = sums

    def z_copy(d):
        return pltpu.make_async_remote_copy(
            src_ref=zsend,
            dst_ref=zbuf.at[z],
            send_sem=z_send,
            recv_sem=z_recv,
            device_id=(ctx, lax.rem(z + d, head_axis)),
            device_id_type=MESH,
        )

    def z_wait(semaphore):
        sample = zbuf.at[pl.ds(0, head_axis - 1)]
        pltpu.make_async_copy(sample, sample, semaphore).wait()

    for d in sorted(range(1, head_axis), key=lambda d: -min(d, head_axis - d)):
        z_copy(d).start()
    sent.append(lambda: z_wait(z_send))
    z_wait(z_recv)
    squares = zbuf[0]
    for other in range(1, head_axis):
        squares = squares + zbuf[other]
    inverse = 1.0 / jnp.sqrt(squares / (heads * head_axis * HD) + 1e-06)
    inverse = jnp.concatenate([inverse, jnp.zeros((HD - 2 * blocks, HD), F32)], axis=0)
    columns = jnp.transpose(inverse)
    for n in range(blocks):
        here = slice(n * HD, (n + 1) * HD)
        scale_a = columns[:, n : n + 1]
        scale_b = columns[:, blocks + n : blocks + n + 1]
        for h in range(heads):
            out[here, h * HD : (h + 1) * HD] = a_buf[h, here, :] * scale_a + b_buf[h, here, :] * scale_b

    for finish in sent:
        finish()


def shards(ctx_count, head_axis, queries, keys, values, head_gain):
    rows = queries.shape[0]
    heads = head_gain.shape[1]
    chips = ctx_count // 2
    half = heads // 2
    each = half // PARTS
    depth = each * HD // chips
    blocks = rows // HD
    anywhere = pl.BlockSpec(memory_space=pl.ANY)
    dma = pltpu.SemaphoreType.DMA
    vmem = pltpu.VMEM
    body = functools.partial(kernel, ctx_count, head_axis, heads, rows)
    return pl.pallas_call(
        body,
        out_shape=pltpu.VMEM((rows, heads * HD), F32),
        in_specs=[anywhere, anywhere, anywhere, pl.BlockSpec(memory_space=pltpu.SMEM)],
        out_specs=pl.BlockSpec(memory_space=pltpu.VMEM),
        scratch_shapes=[
            vmem((heads, rows, HD), F32),
            vmem((heads, rows, HD), F32),
            vmem((heads, rows, HD), F32),
            vmem((heads // 2 - 1, HD, 2 * HD), F32),
            vmem((heads // 2 - 1, HD, 2 * HD), F32),
            vmem((heads // 2, HD, 2 * HD), F32),
            vmem((2, HD, 2 * HD), F32),
            vmem((HD, HD), F32),
            vmem((HD, HD), F32),
            vmem((HD, HD), F32),
            vmem((HD, HD), F32),
            vmem((HD, HD), F32),
            vmem((heads, rows, 2 * HD), BF16),
            vmem((heads, rows, 2 * HD), BF16),
            vmem((heads, rows, 2 * HD), BF16),
            vmem((heads, HD, HD), F32),
            vmem((heads, HD, HD), F32),
            vmem((half, HD, HD), F32),
            vmem((PARTS, each * HD, HD), F32),
            vmem((PARTS, chips, depth, HD), F32),
            vmem((PARTS, chips, depth, HD), F32),
            vmem((PARTS, each * HD, HD), F32),
            vmem((heads, HD, HD), F32),
            vmem((half, HD, HD), F32),
            vmem((heads, rows, HD), F32),
            vmem((heads, rows, HD), F32),
            vmem((rows, HD), F32),
            vmem((rows, HD), F32),
            vmem((2 * blocks, HD), F32),
            vmem((head_axis, 2 * blocks, HD), F32),
            dma((3, heads)),
            dma((2,)),
            dma((2,)),
            dma((heads // 2,)),
            dma((heads // 2,)),
            dma((heads // 2,)),
            dma((heads // 2,)),
            dma,
            dma,
            dma((half,)),
            dma((half,)),
            dma((PARTS,)),
            dma((PARTS,)),
            dma((PARTS,)),
            dma((PARTS,)),
            dma((half,)),
            dma((half,)),
            dma,
            dma,
        ],
        compiler_params=pltpu.CompilerParams(
            collective_id=0, has_side_effects=True, vmem_limit_bytes=60 * 1024 * 1024
        ),
    )(queries, keys, values, head_gain)


def solution(mesh):
    body = functools.partial(shards, mesh.shape["ctx"], mesh.shape["head"])
    in_specs = (P("ctx", "head"), P("ctx", "head"), P("ctx", "head"), P(None, "head"))
    return jax.shard_map(body, mesh=mesh, in_specs=in_specs, out_specs=P("ctx", "head"), check_vma=False)
```

```python
import functools
import math

import jax
import jax.numpy as jnp
from jax import lax
from jax.experimental import pallas as pl
from jax.experimental.pallas import tpu as pltpu
from jax.sharding import PartitionSpec as P

HEADS = 64
HD = 128
WINDOW = 128
MESH = pl.DeviceIdType.MESH
PARTS = 2
START = (("v", 0), ("q", 0), ("q", 1),)
ORDER = (("q", 2), ("i", 0), ("i", 1), ("i", 2), ("i", 3), ("p", 0), ("a", 0), ("i", 4), ("p", 1), ("a", 1), ("a", 2), ("i", 5), ("i", 6), ("i", 7), ("k", 0), ("f", 0), ("f", 1), ("f", 2), ("f", 3),)
F32 = jnp.float32
BF16 = jnp.bfloat16


def split(x):
    high = x.astype(BF16)
    low = (x - high.astype(F32)).astype(BF16)
    return high, low


def dot(a, b, ca, cb):
    return lax.dot_general(a, b, (((ca,), (cb,)), ((), ())), preferred_element_type=F32)


def wide(x):
    both = jnp.concatenate(split(x), axis=1)
    return jnp.concatenate([both, both], axis=0)


def kernel(
    ctx_count, head_axis, heads, rows,
    q_hbm, k_hbm, v_hbm, gain,
    out,
    kbuf, vbuf, qbuf, asked, answer, answered, halo, told, heard, kept, own_peak, own_sum, k2, v2, q2, first, total, pair, chip, gather, prefix, piece_in, state, cross,
    a_buf, b_buf, acc_a, acc_b, zsend, zbuf,
    load_sem, halo_send, halo_recv, ask_send, ask_recv, answer_send, answer_recv, told_send, told_recv, pair_send, pair_recv, gather_send, gather_recv,
    prefix_send, prefix_recv, cross_send, cross_recv, z_send, z_recv,
):
    ctx = lax.axis_index("ctx")
    z = lax.axis_index("head")
    core = lax.rem(ctx, 2)
    mine = lax.div(ctx, 2)
    chips = ctx_count // 2
    half = heads // 2
    each = half // PARTS
    depth = each * HD // chips
    blocks = rows // HD
    factor = 1.0 / math.sqrt(HD)
    sibling = (ctx + 1 - 2 * core, z)
    following = (lax.rem(ctx + 1, ctx_count), z)
    preceding = (lax.rem(ctx + ctx_count - 1, ctx_count), z)
    side = math.isqrt(chips)
    my_y, my_x = lax.div(mine, side), lax.rem(mine, side)
    others = []
    for dy in range(side):
        for dx in range(side):
            hops = min(dx, side - dx) + min(dy, side - dy)
            if hops:
                other = lax.rem(my_y + dy, side) * side + lax.rem(my_x + dx, side)
                others.append((hops, len(others), other))
    others = [other for _, _, other in sorted(others, key=lambda o: (-o[0], o[1]))]

    def piece(c):
        return pl.ds(pl.multiple_of(c * depth, depth), depth)

    def load(source, target, slot, h):
        columns = pl.ds(pl.multiple_of(h * HD, HD), HD)
        return pltpu.make_async_copy(source.at[:, columns], target.at[h], load_sem.at[slot, h])

    sent = []
    has_before = ctx > 0
    has_after = ctx < ctx_count - 1

    def when(condition, *actions):
        @pl.when(condition)
        def _():
            for action in actions:
                action()


    barrier = pltpu.get_barrier_semaphore()

    def greet(device):
        pl.semaphore_signal(barrier, inc=1, device_id=device, device_id_type=MESH)

    for jj in range(heads):
        h = lax.rem(jj + half * (1 - core), heads)
        load(k_hbm, kbuf, 0, h).start()
        load(v_hbm, vbuf, 1, h).start()
    greet(following)
    greet(preceding)
    greet(sibling)
    for other in others:
        greet((2 * other + core, z))
    for d in range(1, head_axis):
        greet((ctx, lax.rem(z + d, head_axis)))
    for h in range(heads):
        load(q_hbm, qbuf, 2, h).start()
    groups = heads // 2 - 1
    last = slice(rows - HD, rows)

    def ask_copy(g):
        return pltpu.make_async_remote_copy(
            src_ref=q_hbm.at[pl.ds(0, HD), pl.ds(pl.multiple_of(g * 2 * HD, HD), 2 * HD)],
            dst_ref=asked.at[g],
            send_sem=ask_send.at[g],
            recv_sem=ask_recv.at[g],
            device_id=preceding,
            device_id_type=MESH,
        )

    def answer_copy(g):
        return pltpu.make_async_remote_copy(
            src_ref=answer.at[g],
            dst_ref=answered.at[g],
            send_sem=answer_send.at[g],
            recv_sem=answer_recv.at[g],
            device_id=following,
            device_id_type=MESH,
        )

    kept_columns = pl.ds(groups * 2 * HD, 2 * HD)

    def halo_copy(slot):
        return pltpu.make_async_remote_copy(
            src_ref=(k_hbm, v_hbm)[slot].at[pl.ds(rows - HD, HD), kept_columns],
            dst_ref=halo.at[slot],
            send_sem=halo_send.at[slot],
            recv_sem=halo_recv.at[slot],
            device_id=following,
            device_id_type=MESH,
        )

    def send_halo(_):
        when(has_after, *[halo_copy(slot).start for slot in range(2)])

    def ask(g):
        when(has_before, ask_copy(g).start)

    def told_copy():
        return pltpu.make_async_remote_copy(
            src_ref=told,
            dst_ref=heard,
            send_sem=told_send,
            recv_sem=told_recv,
            device_id=following,
            device_id_type=MESH,
        )

    def local_state(h):
        load(k_hbm, kbuf, 0, h).wait()
        load(v_hbm, vbuf, 1, h).wait()
        k_high, k_low = split(kbuf[h])
        v_high, v_low = split(vbuf[h])
        k2[h, :, :HD] = k_high
        k2[h, :, HD:] = k_low
        v2[h, :, :HD] = v_high
        v2[h, :, HD:] = v_low
        kk = jnp.concatenate([k_high, k_low], axis=1)
        vv = jnp.concatenate([v_high, v_low], axis=1)
        mid = rows // 2
        parts = []
        for part in range(2):
            r = dot(kk[part * mid : (part + 1) * mid], vv[part * mid : (part + 1) * mid], 0, 0)
            parts.append(r[:HD, :HD] + (r[:HD, HD:] + r[HD:, :HD]))
        first[h] = parts[0]
        total[h] = parts[0] + parts[1]

    def pair_copy(j):
        return pltpu.make_async_remote_copy(
            src_ref=total.at[half * (1 - core) + j],
            dst_ref=pair.at[j],
            send_sem=pair_send.at[j],
            recv_sem=pair_recv.at[j],
            device_id=sibling,
            device_id_type=MESH,
        )

    def gather_copy(j, target):
        return pltpu.make_async_remote_copy(
            src_ref=chip.at[j, piece(target), :],
            dst_ref=gather.at[j, mine],
            send_sem=gather_send.at[j],
            recv_sem=gather_recv.at[j],
            device_id=(2 * target + core, z),
            device_id_type=MESH,
        )

    def prefix_copy(j, target):
        return pltpu.make_async_remote_copy(
            src_ref=prefix.at[j, target],
            dst_ref=piece_in.at[j, piece(mine), :],
            send_sem=prefix_send.at[j],
            recv_sem=prefix_recv.at[j],
            device_id=(2 * target + core, z),
            device_id_type=MESH,
        )

    def all_others(semaphore):
        sample = gather.at[0, pl.ds(0, chips - 1)]
        pltpu.make_async_copy(sample, sample, semaphore).wait()

    @pl.loop(0, half)
    def _(j):
        local_state(half * (1 - core) + j)

    pl.semaphore_wait(barrier, 3 + chips - 1 + head_axis - 1)
    for j in range(half):
        pair_copy(j).start()
    for name, which in START:
        {"v": send_halo, "q": ask}[name](which)
    sent.append(lambda: when(has_before, *[ask_copy(g).wait_send for g in range(groups)]))
    sent.append(lambda: when(has_after, *[halo_copy(slot).wait_send for slot in range(2)]))

    def pair_done():
        @pl.loop(0, half)
        def _(j):
            pair_copy(j).wait_send()

    sent.append(pair_done)

    @pl.loop(0, PARTS)
    def _(p):
        for e in range(each):
            j = p * each + e
            h = half * core + j
            local_state(h)
            pair_copy(j).wait_recv()
            chip[p, e * HD : (e + 1) * HD, :] = total[h] + pair[j]
        gather[p, mine] = chip[p, piece(mine), :]
        for other in others:
            gather_copy(p, other).start()

    def gather_done():
        @pl.loop(0, PARTS)
        def _(p):
            all_others(gather_send.at[p])

    sent.append(gather_done)
    row = lax.broadcasted_iota(jnp.int32, (HD, 2 * HD), 0)
    col = lax.broadcasted_iota(jnp.int32, (HD, 2 * HD), 1)
    band = (col > row) & (col <= row + HD)
    causal_even = (col >= HD) & (col <= row + HD)
    causal_odd = col <= row + HD
    lane = col[:, :HD]
    lower = lane <= row[:, :HD]

    acc_a[...] = jnp.zeros_like(acc_a)
    acc_b[...] = jnp.zeros_like(acc_b)
    told[...] = jnp.zeros_like(told)
    kept[...] = jnp.zeros_like(kept)
    own_peak[...] = jnp.zeros_like(own_peak)

    @pl.when(ctx == 0)
    def _():
        answered[...] = jnp.zeros_like(answered)
        heard[...] = jnp.zeros_like(heard)
        halo[...] = jnp.zeros_like(halo)

    @pl.when(ctx == ctx_count - 1)
    def _():
        asked[...] = jnp.zeros_like(asked)

    own_sum[...] = jnp.zeros_like(own_sum)

    def scores(q_low_high, keys):
        return dot(q_low_high[:, HD:], keys[:, :HD], 1, 1) + dot(q_low_high, keys, 1, 1)

    def block(h, n):
        here = slice(n * HD, (n + 1) * HD)
        both = slice(max(n - 1, 0) * HD, (n + 1) * HD)
        allowed = band if n else lower
        causal = (causal_odd if n % 2 else causal_even) if n else lower
        s = scores(q2[h, here, :], k2[h, both, :])
        masked = jnp.where(allowed, s, -jnp.inf)
        biggest = jnp.max(masked, axis=1, keepdims=True)
        weights = jnp.exp((masked - biggest) * factor)
        weight_sum = jnp.sum(weights, axis=1, keepdims=True)
        inner = jnp.where(causal, s, 0.0)
        stacked = jnp.concatenate(split(weights) + split(inner), axis=0)
        r = dot(stacked, v2[h, both, :], 1, 0)
        win = r[:HD, :HD] + (r[:HD, HD:] + r[HD : 2 * HD, :HD])
        lin = r[2 * HD : 3 * HD, :HD] + (r[2 * HD : 3 * HD, HD:] + r[3 * HD :, :HD])
        if n:
            a = win * (gain[0, h] / weight_sum)
            a_buf[h, here, :] = a
            acc_a[here, :] += a * a
        else:
            a_buf[h, here, :] = win
            own_peak[...] = jnp.where(lane == h, biggest, own_peak[...])
            own_sum[...] = jnp.where(lane == h, weight_sum, own_sum[...])
        return lin

    def inner_blocks(h):
        load(q_hbm, qbuf, 2, h).wait()
        q_high, q_low = split(qbuf[h])
        q2[h, :, :HD] = q_low
        q2[h, :, HD:] = q_high
        mid = rows // 2
        carried = dot(q2[h, mid:, :], wide(first[h]), 1, 0)
        carried = carried[:, :HD] + carried[:, HD:]
        for n in range(blocks):
            lin = block(h, n)
            if n * HD >= mid:
                lin = lin + carried[n * HD - mid : (n + 1) * HD - mid]
            b_buf[h, n * HD : (n + 1) * HD, :] = lin

    def partial(h, q_high, q_low, keys, vals, target, tile):
        s = scores(jnp.concatenate([q_low, q_high], axis=1), keys)
        biggest = jnp.max(jnp.where(lower, -3e38, s), axis=1, keepdims=True)
        weights = jnp.where(lower, 0.0, jnp.exp((s - biggest) * factor))
        weight_sum = jnp.sum(weights, axis=1, keepdims=True)
        r = dot(jnp.concatenate(split(weights), axis=0), vals, 1, 0)
        target[:, h % 2 * HD : (h % 2 + 1) * HD] = r[:HD, :HD] + (r[:HD, HD:] + r[HD:, :HD])
        tile[...] = jnp.where(lane == h, biggest, jnp.where(lane == heads + h, weight_sum, tile[...]))

    def answer_group(g):
        when(has_after, ask_copy(g).wait_recv)
        for h in (2 * g, 2 * g + 1):
            q_high, q_low = split(asked[g, :, h % 2 * HD : (h % 2 + 1) * HD])
            partial(h, q_high, q_low, k2[h, last, :], v2[h, last, :], answer.at[g], told)
        when(has_after, answer_copy(g).start)

    def keep_group(_):
        when(has_before, *[halo_copy(slot).wait_recv for slot in range(2)])
        for h in (2 * groups, 2 * groups + 1):
            columns = slice(h % 2 * HD, (h % 2 + 1) * HD)
            keys = jnp.concatenate(split(halo[0, :, columns]), axis=1)
            vals = jnp.concatenate(split(halo[1, :, columns]), axis=1)
            q_low_high = q2[h, :HD, :]
            partial(h, q_low_high[:, HD:], q_low_high[:, :HD], keys, vals, answered.at[groups], kept)

    def return_prefixes(j):
        all_others(gather_recv.at[j])
        running = jnp.zeros((depth, HD), F32)
        for c in range(chips):
            prefix[j, c] = running
            if c < chips - 1:
                running = running + gather[j, c]
        piece_in[j, piece(mine), :] = prefix[j, mine]
        for other in others:
            prefix_copy(j, other).start()

    def prefix_done():
        @pl.loop(0, PARTS)
        def _(p):
            all_others(prefix_send.at[p])

    sent.append(prefix_done)

    def cross_copy(j):
        return pltpu.make_async_remote_copy(
            src_ref=cross.at[j],
            dst_ref=state.at[half * core + j],
            send_sem=cross_send.at[j],
            recv_sem=cross_recv.at[j],
            device_id=sibling,
            device_id_type=MESH,
        )

    def forward(j):
        h = half * core + j
        p, e = j // each, j % each
        if e == 0:
            all_others(prefix_recv.at[p])
        before = piece_in[p, e * HD : (e + 1) * HD, :]
        state[h] = before + jnp.where(core == 1, pair[j], 0.0)
        cross[j] = before + jnp.where(core == 0, total[h], 0.0)
        cross_copy(j).start()

    def inner_pair(h):
        @pl.loop(h, h + 2)
        def _(each):
            inner_blocks(each)

    steps = {"v": send_halo, "k": keep_group, "q": ask, "i": inner_blocks, "d": inner_pair, "a": answer_group, "p": return_prefixes, "f": forward}
    for name, which in ORDER:
        steps[name](which)

    def cross_done():
        @pl.loop(0, half)
        def _(j):
            cross_copy(j).wait_send()

    sent.append(cross_done)

    def answer_done():
        when(has_after, told_copy().wait_send, *[answer_copy(g).wait_send for g in range(groups)])

    when(has_after, told_copy().start)
    sent.append(answer_done)

    def merge():
        when(has_before, told_copy().wait_recv, *[answer_copy(g).wait_recv for g in range(groups)])
        peak = own_peak[...]
        other = heard[...] + kept[...]
        other_peak = jnp.where(ctx > 0, other, -3e38)
        other_sum = pltpu.roll(other, HD - heads, 1)
        biggest = jnp.maximum(peak, other_peak)
        scale = jnp.exp((peak - biggest) * factor)
        other_scale = jnp.where(ctx > 0, jnp.exp((other_peak - biggest) * factor), 0.0)
        whole = own_sum[...] * scale + other_sum * other_scale
        scale = scale / whole
        other_scale = other_scale / whole
        square = acc_a[:HD, :]
        for h in range(heads):
            columns = slice(h % 2 * HD, (h % 2 + 1) * HD)
            a = a_buf[h, :HD, :] * scale[:, h : h + 1]
            a = (a + answered[h // 2, :, columns] * other_scale[:, h : h + 1]) * gain[0, h]
            a_buf[h, :HD, :] = a
            square = square + a * a
        acc_a[:HD, :] = square

    def last_linear(h):
        r = dot(q2[h], wide(state[h]), 1, 0)
        b = (b_buf[h] + (r[:, :HD] + r[:, HD:])) * gain[1, h]
        b_buf[h] = b
        acc_b[...] += b * b

    @pl.loop(0, half)
    def _(j):
        last_linear(half * core + j)

    @pl.loop(0, half)
    def _(j):
        cross_copy(j).wait_recv()
        last_linear(half * (1 - core) + j)

    def block_sum(acc, n):
        return jnp.sum(jnp.transpose(acc[n * HD : (n + 1) * HD, :]), axis=0, keepdims=True)

    sums = [block_sum(acc_a, n) for n in range(1, blocks)] + [block_sum(acc_b, n) for n in range(blocks)]
    zsend[1:, :] = jnp.concatenate(sums, axis=0)
    merge()
    zsend[:1, :] = block_sum(acc_a, 0)
    sums = zsend[...]
    zbuf[z] = sums

    def z_copy(d):
        return pltpu.make_async_remote_copy(
            src_ref=zsend,
            dst_ref=zbuf.at[z],
            send_sem=z_send,
            recv_sem=z_recv,
            device_id=(ctx, lax.rem(z + d, head_axis)),
            device_id_type=MESH,
        )

    def z_wait(semaphore):
        sample = zbuf.at[pl.ds(0, head_axis - 1)]
        pltpu.make_async_copy(sample, sample, semaphore).wait()

    for d in sorted(range(1, head_axis), key=lambda d: -min(d, head_axis - d)):
        z_copy(d).start()
    sent.append(lambda: z_wait(z_send))
    z_wait(z_recv)
    squares = zbuf[0]
    for other in range(1, head_axis):
        squares = squares + zbuf[other]
    inverse = 1.0 / jnp.sqrt(squares / (heads * head_axis * HD) + 1e-06)
    inverse = jnp.concatenate([inverse, jnp.zeros((HD - 2 * blocks, HD), F32)], axis=0)
    columns = jnp.transpose(inverse)
    for n in range(blocks):
        here = slice(n * HD, (n + 1) * HD)
        scale_a = columns[:, n : n + 1]
        scale_b = columns[:, blocks + n : blocks + n + 1]
        for h in range(heads):
            out[here, h * HD : (h + 1) * HD] = a_buf[h, here, :] * scale_a + b_buf[h, here, :] * scale_b

    for finish in sent:
        finish()


def shards(ctx_count, head_axis, queries, keys, values, head_gain):
    rows = queries.shape[0]
    heads = head_gain.shape[1]
    chips = ctx_count // 2
    half = heads // 2
    each = half // PARTS
    depth = each * HD // chips
    blocks = rows // HD
    anywhere = pl.BlockSpec(memory_space=pl.ANY)
    dma = pltpu.SemaphoreType.DMA
    vmem = pltpu.VMEM
    body = functools.partial(kernel, ctx_count, head_axis, heads, rows)
    return pl.pallas_call(
        body,
        out_shape=pltpu.VMEM((rows, heads * HD), F32),
        in_specs=[anywhere, anywhere, anywhere, pl.BlockSpec(memory_space=pltpu.SMEM)],
        out_specs=pl.BlockSpec(memory_space=pltpu.VMEM),
        scratch_shapes=[
            vmem((heads, rows, HD), F32),
            vmem((heads, rows, HD), F32),
            vmem((heads, rows, HD), F32),
            vmem((heads // 2 - 1, HD, 2 * HD), F32),
            vmem((heads // 2 - 1, HD, 2 * HD), F32),
            vmem((heads // 2, HD, 2 * HD), F32),
            vmem((2, HD, 2 * HD), F32),
            vmem((HD, HD), F32),
            vmem((HD, HD), F32),
            vmem((HD, HD), F32),
            vmem((HD, HD), F32),
            vmem((HD, HD), F32),
            vmem((heads, rows, 2 * HD), BF16),
            vmem((heads, rows, 2 * HD), BF16),
            vmem((heads, rows, 2 * HD), BF16),
            vmem((heads, HD, HD), F32),
            vmem((heads, HD, HD), F32),
            vmem((half, HD, HD), F32),
            vmem((PARTS, each * HD, HD), F32),
            vmem((PARTS, chips, depth, HD), F32),
            vmem((PARTS, chips, depth, HD), F32),
            vmem((PARTS, each * HD, HD), F32),
            vmem((heads, HD, HD), F32),
            vmem((half, HD, HD), F32),
            vmem((heads, rows, HD), F32),
            vmem((heads, rows, HD), F32),
            vmem((rows, HD), F32),
            vmem((rows, HD), F32),
            vmem((2 * blocks, HD), F32),
            vmem((head_axis, 2 * blocks, HD), F32),
            dma((3, heads)),
            dma((2,)),
            dma((2,)),
            dma((heads // 2,)),
            dma((heads // 2,)),
            dma((heads // 2,)),
            dma((heads // 2,)),
            dma,
            dma,
            dma((half,)),
            dma((half,)),
            dma((PARTS,)),
            dma((PARTS,)),
            dma((PARTS,)),
            dma((PARTS,)),
            dma((half,)),
            dma((half,)),
            dma,
            dma,
        ],
        compiler_params=pltpu.CompilerParams(
            collective_id=0, has_side_effects=True, vmem_limit_bytes=60 * 1024 * 1024
        ),
    )(queries, keys, values, head_gain)


def solution(mesh):
    body = functools.partial(shards, mesh.shape["ctx"], mesh.shape["head"])
    in_specs = (P("ctx", "head"), P("ctx", "head"), P("ctx", "head"), P(None, "head"))
    return jax.shard_map(body, mesh=mesh, in_specs=in_specs, out_specs=P("ctx", "head"), check_vma=False)
```
